512 devices in a mesh: member: 16 (over y_lo, x), space: 32 (over y_hi, z, core).
Axes of the slice: x: 4, y: 8 (y_hi: 2, y_lo: 4; y = y_hi * 4 + y_lo), z: 8, core: 2. Of those that a mesh axis runs over, the one named last changes fastest.
Arguments:
- ensemble: float32 [128, 64, 64, 128], P(None, 'space', 'member'), may hold values from -4 to 4
- source: float32 [64, 64, 128], P('space', 'member'), may hold values from -6 to 6
- obs_rows: int32 [32, 16, 1], P('space', 'member'), may hold values from 0 to 7
- obs_values: float32 [32, 16, 128], P('space', 'member'), may hold values from -3 to 3
- obs_noise: float32 [128, 32, 16, 128], P(None, 'space', 'member'), may hold values from -5 to 5
- obs_var: float32 [32, 16, 128], P('space', 'member'), may hold values from 0.05 to 2
Outputs:
- updated: float32 [128, 64, 64, 128], P(None, 'space', 'member')
- predicted: float32 [128, 32, 16, 128], P(None, 'space', 'member')
The draws below stay inside these ranges and needn't reach their ends.
Inputs may be any that keep to these rules, and one draw needn't show every extreme that they name: `obs_rows`: entry [s, m, o] names the cell row at (s * 2 + r // 4, m * 4 + r % 4) of the first two dimensions, whose 128 cells along the third dimension are observed; rows may repeat.
All inputs are finite; a program needn't handle non-finite values.
Results may differ from the reference program's by a relative error of at most 0.0003.
Values sent between devices are 32-bit elements; how exact they have to be, the bound alone decides.
A program may use at most 64 MiB of HBM per device.

```python
import math
import jax
import jax.numpy as jnp
from jax import lax

M = 128
CX = 2
CY = 4
NZ = 128
OBS_DEV = 1
ITERS = 4
NX = 64
NY = 64
N_MEMBER = 16
N_SPACE = 32


def with_ends(drawn, key, least, largest):
    index_at = [jax.random.randint(jax.random.fold_in(key, axis), (), 0, length) for axis, length in enumerate(drawn.shape)]
    longest = drawn.shape.index(max(drawn.shape))
    next_to = index_at[:longest] + [(index_at[longest] + 1) % drawn.shape[longest]] + index_at[longest + 1:]
    return drawn.at[tuple(index_at)].set(least).at[tuple(next_to)].set(largest)


def levels(key, shape, split, smallest, top_value):
    loudness, own = 1.0, jax.random.fold_in(key, 6)
    for dim, blocks in split:
        draws = jnp.exp(jax.random.uniform(jax.random.fold_in(own, dim), (blocks,), jnp.float32, smallest / len(split), top_value / len(split)))
        loudness = loudness * jnp.repeat(draws, shape[dim] // blocks).reshape([-1 if axis == dim else 1 for axis in range(len(shape))])
    return loudness


def centred(stream_key, dims, scale, bound, cuts=(), kind=jnp.bfloat16):
    array = scale * jax.random.normal(stream_key, dims, jnp.float32)
    if cuts:
        array = array * levels(stream_key, dims, cuts, -0.22, 0.18)
    return jnp.clip(array, -bound, bound).astype(kind)


def setup_inputs(seed: int = 0) -> dict:
    arg_keys = jax.random.split(jax.random.key(seed), 7)
    ensemble = centred(arg_keys[0], (M, NX, NY, NZ), 1.0, 4.0, ((1, 32), (2, 16)), jnp.float32)
    source = centred(arg_keys[1], (NX, NY, NZ), 1.0, 6.0, ((0, 32), (1, 16)), jnp.float32)
    obs_rows = with_ends(jax.random.randint(arg_keys[2], (N_SPACE, N_MEMBER, OBS_DEV), 0, CX * CY), jax.random.fold_in(arg_keys[2], 1), 0, (CX * CY) - 1).astype(jnp.int32)
    obs_values = centred(arg_keys[3], (N_SPACE, N_MEMBER, OBS_DEV * NZ), 0.5, 3.0, ((0, 32), (1, 16)), jnp.float32)
    obs_noise = centred(arg_keys[4], (M, N_SPACE, N_MEMBER, OBS_DEV * NZ), 1.0, 5.0, ((1, 32), (2, 16)), jnp.float32)
    obs_var = jnp.clip(jnp.exp(math.log(2.0) - 3.6888794 * jax.random.uniform(arg_keys[5], (N_SPACE, N_MEMBER, OBS_DEV * NZ), jnp.float32) ** levels(arg_keys[5], (N_SPACE, N_MEMBER, OBS_DEV * NZ), ((0, 32), (1, 16)), -0.2, 0.2)), 0.05, 2.0)
    return {"ensemble": ensemble, "source": source, "obs_rows": obs_rows, "obs_values": obs_values, "obs_noise": obs_noise, "obs_var": obs_var}


def harmonic(first_cond, second_cond):
    return 2.0 * first_cond * second_cond / (first_cond + second_cond)

def face_terms(cond):
    cond_pad = jnp.pad(cond, 1, mode='edge')
    face_x = harmonic(cond_pad[:-1, 1:-1, 1:-1], cond_pad[1:, 1:-1, 1:-1])
    face_y = harmonic(cond_pad[1:-1, :-1, 1:-1], cond_pad[1:-1, 1:, 1:-1])
    face_z = harmonic(cond, cond_pad[1:-1, 1:-1, 2:])
    lower_z = jnp.concatenate([harmonic(cond[..., :1], cond[..., :1]), face_z[..., :-1]], axis=-1)
    return (face_x, face_y, face_z, lower_z)

def operate(values_in, face_x, face_y, face_z, lower_z):
    padded = jnp.pad(values_in, 1)
    result = face_x[1:] * (values_in - padded[2:, 1:-1, 1:-1]) + face_x[:-1] * (values_in - padded[:-2, 1:-1, 1:-1])
    result = result + face_y[:, 1:] * (values_in - padded[1:-1, 2:, 1:-1]) + face_y[:, :-1] * (values_in - padded[1:-1, :-2, 1:-1])
    result = result + face_z * (values_in - padded[1:-1, 1:-1, 2:]) + lower_z * (values_in - padded[1:-1, 1:-1, :-2])
    return result

def conjugate(cond, source):
    face_x, face_y, face_z, lower_z = face_terms(cond)
    residual = source
    direction = source
    solution = jnp.zeros_like(source)
    norm_now = jnp.sum(residual * residual)
    for iteration in range(ITERS):
        image = operate(direction, face_x, face_y, face_z, lower_z)
        step_size = norm_now / jnp.sum(direction * image)
        solution = solution + step_size * direction
        residual = residual - step_size * image
        if iteration + 1 < ITERS:
            norm_next = jnp.sum(residual * residual)
            direction = residual + norm_next / norm_now * direction
            norm_now = norm_next
    return solution

def reference(ensemble, source, obs_rows, obs_values, obs_noise, obs_var):
    slab_ids = jnp.arange(N_SPACE).astype(jnp.int32)[:, None, None]
    column_ids = jnp.arange(N_MEMBER).astype(jnp.int32)[None, :, None]
    cell_x = slab_ids * CX + obs_rows // CY
    cell_y = column_ids * CY + obs_rows % CY

    def member_pred(member_field):
        pressure = conjugate(jnp.exp(member_field), source)
        return pressure[cell_x, cell_y, :].reshape(N_SPACE, N_MEMBER, OBS_DEV * NZ)
    predicted = lax.map(member_pred, ensemble)
    flat_pred = predicted.reshape(M, -1)
    inv_sigma = 1.0 / jnp.sqrt(obs_var.reshape(-1))
    spread = (flat_pred - lax.optimization_barrier(jnp.mean(flat_pred, axis=0))) * inv_sigma
    misfit = (obs_values.reshape(-1) - flat_pred) * inv_sigma + obs_noise.reshape(M, -1)
    gram_sum = jnp.dot(spread, spread.T, precision=lax.Precision.HIGHEST)
    cross_sum = jnp.dot(spread, misfit.T, precision=lax.Precision.HIGHEST)
    factor = jnp.linalg.cholesky(gram_sum + (M - 1.0) * jnp.eye(M, dtype=jnp.float32))
    weights = jax.scipy.linalg.cho_solve((factor, True), cross_sum)
    flat_field = ensemble.reshape(M, -1)
    anomalies = flat_field - lax.optimization_barrier(jnp.mean(flat_field, axis=0))
    updated = flat_field + jnp.dot(weights.T, anomalies, precision=lax.Precision.HIGHEST)
    return (updated.reshape(ensemble.shape), predicted)
```

```python
import jax
import jax.numpy as jnp
from jax import lax
from jax.experimental import pallas as pl
from jax.experimental.pallas import tpu as pltpu
from jax.sharding import PartitionSpec as P

X, Y_LO, Y_HI, Z, CORES = 4, 4, 2, 8, 2
WIDE = 8

ITERS = 4


def padded_2(x, sides, width):
    for axis, dim in sides:
        devices, length = (lax.axis_size(axis), x.shape[dim])
        up = [(i, (i + 1) % devices) for i in range(devices - 1)]
        down = [(j, i) for i, j in up]
        last = lax.slice_in_dim(x, length - width, length, axis=dim)
        leading = lax.slice_in_dim(x, 0, width, axis=dim)
        before = lax.ppermute(last, axis, up)
        after = lax.ppermute(leading, axis, down)
        x = jnp.concatenate([before, x, after], axis=dim)
    return x


def from_everyone(x, axis):
    devices = lax.axis_size(axis)
    return lax.all_to_all(jnp.broadcast_to(x[None], (devices, *x.shape)), axis, 0, 0, tiled=True)


def over_copies(x, axis):
    everything = from_everyone(x, axis)
    return jnp.sum(everything, axis=0)


def joined_along(pieces, dim):
    shape = list(pieces.shape[1:])
    shape[dim] *= pieces.shape[0]
    return jnp.moveaxis(pieces, 0, dim).reshape(shape)


def collect(x, axis, dim):
    pieces = from_everyone(x, axis)
    return joined_along(pieces, dim)


def place():
    member = lax.axis_index("member")
    space = lax.axis_index("space")
    x = lax.rem(member, X)
    y = lax.div(space, Z * CORES) * Y_LO + lax.div(member, X)
    z = lax.rem(lax.div(space, CORES), Z)
    return x, y, z, lax.rem(space, CORES)


def device_at(x, y, z, core):
    member = lax.rem(y, Y_LO) * X + x
    space = (lax.div(y, Y_LO) * Z + z) * CORES + core
    return {"member": member, "space": space}


def sum_kernel(part, total, got_row, sum_row, got_y, sum_y, got_z, all_y, all_row, send_sems, recv_sems):
    x, y, z, core = place()
    row = x * CORES + core

    def row_peer(step):
        other = lax.rem(row + step, WIDE)
        return other, device_at(lax.div(other, CORES), y, z, lax.rem(other, CORES))

    def y_peer(step):
        other = lax.rem(y + step, WIDE)
        return other, device_at(x, other, z, core)

    def z_peer(step):
        other = lax.rem(z + step, WIDE)
        return other, device_at(x, y, other, core)

    barrier = pltpu.get_barrier_semaphore()
    for peer in (row_peer, y_peer, z_peer):
        for step in range(1, WIDE):
            pl.semaphore_signal(barrier, inc=1, device_id=peer(step)[1], device_id_type=pl.DeviceIdType.MESH)
    pl.semaphore_wait(barrier, 3 * (WIDE - 1))

    def exchange(phase, peer, source, target):
        copies = []
        for step in range(1, WIDE):
            other, device = peer(step)
            copy = pltpu.make_async_remote_copy(
                src_ref=source(other),
                dst_ref=target(step),
                send_sem=send_sems.at[phase, step - 1],
                recv_sem=recv_sems.at[phase, step - 1],
                device_id=device,
                device_id_type=pl.DeviceIdType.MESH,
            )
            copy.start()
            copies.append(copy)
        return copies

    def arrived(copies):
        for copy in copies:
            copy.wait_recv()

    sent = []
    copies = exchange(0, row_peer, lambda o: part.at[pl.ds(o * WIDE, WIDE)], lambda s: got_row.at[s - 1])
    sent += copies
    arrived(copies)
    sum_row[...] = part[pl.ds(row * WIDE, WIDE)] + jnp.sum(got_row[...], axis=0)

    copies = exchange(1, y_peer, lambda o: sum_row.at[o], lambda s: got_y.at[s - 1])
    sent += copies
    arrived(copies)
    sum_y[...] = sum_row[y] + jnp.sum(got_y[...], axis=0)

    got_z[z] = sum_y[...]
    copies = exchange(2, z_peer, lambda o: sum_y, lambda s: got_z.at[z])
    sent += copies
    arrived(copies)
    sum_y_z = jnp.sum(got_z[...], axis=0)
    all_y[y] = sum_y_z

    copies = exchange(3, y_peer, lambda o: all_y.at[y], lambda s: all_y.at[y])
    sent += copies
    arrived(copies)

    copies = exchange(4, row_peer, lambda o: all_y, lambda s: all_row.at[row])
    sent += copies
    all_row[row] = all_y[...]
    arrived(copies)
    total[...] = all_row[...].reshape(total.shape)
    for copy in sent:
        copy.wait_send()


def sum_everywhere(part):
    dims = part.shape[1:]
    return pl.pallas_call(
        sum_kernel,
        out_shape=jax.ShapeDtypeStruct(part.shape, jnp.float32),
        in_specs=[pl.BlockSpec(memory_space=pltpu.VMEM)],
        out_specs=pl.BlockSpec(memory_space=pltpu.VMEM),
        scratch_shapes=[
            pltpu.VMEM((WIDE - 1, WIDE, *dims), jnp.float32),
            pltpu.VMEM((WIDE, *dims), jnp.float32),
            pltpu.VMEM((WIDE - 1, *dims), jnp.float32),
            pltpu.VMEM(dims, jnp.float32),
            pltpu.VMEM((WIDE, *dims), jnp.float32),
            pltpu.VMEM((WIDE, *dims), jnp.float32),
            pltpu.VMEM((WIDE, WIDE, *dims), jnp.float32),
            pltpu.SemaphoreType.DMA((5, WIDE - 1)),
            pltpu.SemaphoreType.DMA((5, WIDE - 1)),
        ],
        compiler_params=pltpu.CompilerParams(collective_id=1, has_side_effects=True),
        name="sum_everywhere",
    )(part)


def harmonic(first_cond, second_cond):
    return 2.0 * first_cond * second_cond / (first_cond + second_cond)


def extend_cond(cond):
    widened = padded_2(cond, (("member", 2),), 1)
    return jnp.pad(widened, ((0, 0), (1, 1), (0, 0), (1, 1)))


def extend_values(values_in):
    widened = padded_2(values_in, (("member", 2),), 1)
    return jnp.pad(widened, ((0, 0), (1, 1), (0, 0), (1, 1)))


def member_dots(dot_terms):
    return over_copies(dot_terms, "member")


def face_terms(cond):
    widened = extend_cond(cond)
    edge_pad = jnp.pad(cond, ((0, 0), (1, 1), (1, 1), (1, 1)), mode="edge")
    cond_pad = jnp.where(widened > 0.0, widened, edge_pad)
    face_x = harmonic(cond_pad[:, :-1, 1:-1, 1:-1], cond_pad[:, 1:, 1:-1, 1:-1])
    face_y = harmonic(cond_pad[:, 1:-1, :-1, 1:-1], cond_pad[:, 1:-1, 1:, 1:-1])
    face_z = harmonic(cond, cond_pad[:, 1:-1, 1:-1, 2:])
    lower_z = jnp.concatenate([harmonic(cond[..., :1], cond[..., :1]), face_z[..., :-1]], axis=-1)
    return (face_x, face_y, face_z, lower_z)


def operate(values_in, face_x, face_y, face_z, lower_z):
    padded = extend_values(values_in)
    result = face_x[:, 1:] * (values_in - padded[:, 2:, 1:-1, 1:-1]) + face_x[:, :-1] * (
        values_in - padded[:, :-2, 1:-1, 1:-1]
    )
    result = (
        result
        + face_y[:, :, 1:] * (values_in - padded[:, 1:-1, 2:, 1:-1])
        + face_y[:, :, :-1] * (values_in - padded[:, 1:-1, :-2, 1:-1])
    )
    result = (
        result
        + face_z * (values_in - padded[:, 1:-1, 1:-1, 2:])
        + lower_z * (values_in - padded[:, 1:-1, 1:-1, :-2])
    )
    return result


def conjugate(cond, forcing):
    face_x, face_y, face_z, lower_z = face_terms(cond)
    residual = jnp.broadcast_to(forcing[None], cond.shape)
    direction = residual
    solution = jnp.zeros_like(cond)
    norm_now = member_dots(jnp.sum(residual * residual, axis=(1, 2, 3)))
    for iteration in range(ITERS):
        image = operate(direction, face_x, face_y, face_z, lower_z)
        step_size = norm_now / member_dots(jnp.sum(direction * image, axis=(1, 2, 3)))
        solution = solution + step_size[:, None, None, None] * direction
        residual = residual - step_size[:, None, None, None] * image
        if iteration + 1 < ITERS:
            norm_next = member_dots(jnp.sum(residual * residual, axis=(1, 2, 3)))
            direction = residual + (norm_next / norm_now)[:, None, None, None] * direction
            norm_now = norm_next
    return solution


def local(ensemble, source, obs_rows, obs_values, obs_noise, obs_var):
    total_members = ensemble.shape[0]
    block_x, block_y, layers = source.shape
    held_fields = lax.all_to_all(ensemble, "space", split_axis=0, concat_axis=1, tiled=True)
    forcing = collect(source, "space", 0)
    pressure = conjugate(jnp.exp(held_fields), forcing)
    held_count = pressure.shape[0]
    cells_flat = pressure.reshape(held_count, -1, layers)
    gathered_rows = collect(obs_rows, "space", 0)
    row_ids = gathered_rows[:, 0]
    peer_ids = jnp.arange(row_ids.shape[0], dtype=jnp.int32)[:, None]
    flat_index = (peer_ids * block_x + row_ids // block_y) * block_y + row_ids % block_y
    picked = jnp.take(cells_flat, flat_index.reshape(-1), axis=1)
    returned = lax.all_to_all(picked, "space", split_axis=1, concat_axis=0, tiled=True)
    predicted = returned.reshape(total_members, 1, 1, -1)
    flat_pred = returned.reshape(total_members, -1)
    inv_sigma = 1.0 / jnp.sqrt(obs_var.reshape(-1))
    spread = (flat_pred - jnp.mean(flat_pred, axis=0)) * inv_sigma
    misfit = (obs_values.reshape(-1) - flat_pred) * inv_sigma + obs_noise.reshape(total_members, -1)
    gram_part = jnp.dot(spread, spread.T, precision=lax.Precision.HIGHEST)
    cross_part = jnp.dot(spread, misfit.T, precision=lax.Precision.HIGHEST)
    both = sum_everywhere(jnp.concatenate([gram_part, cross_part]).reshape(64, 4, -1))
    gram_sum, cross_sum = jnp.split(both.reshape(2 * total_members, total_members), 2)
    factor = jnp.linalg.cholesky(
        gram_sum + (total_members - 1.0) * jnp.eye(total_members, dtype=jnp.float32)
    )
    weights = jax.scipy.linalg.cho_solve((factor, True), cross_sum)
    flat_field = ensemble.reshape(total_members, -1)
    anomalies = flat_field - jnp.mean(flat_field, axis=0)
    updated = flat_field + jnp.dot(weights.T, anomalies, precision=lax.Precision.HIGHEST)
    return (updated.reshape(ensemble.shape), predicted)


def solution(mesh):
    in_specs = (
        P(None, "space", "member", None),
        P("space", "member", None),
        P("space", "member", None),
        P("space", "member", None),
        P(None, "space", "member", None),
        P("space", "member", None),
    )
    out_specs = (P(None, "space", "member", None), P(None, "space", "member", None))
    return jax.shard_map(local, mesh=mesh, in_specs=in_specs, out_specs=out_specs, check_vma=False)
```

```python
import jax
import jax.numpy as jnp
from jax import lax
from jax.experimental import pallas as pl
from jax.experimental.pallas import tpu as pltpu
from jax.sharding import PartitionSpec as P

X, Y_LO, Y_HI, Z, CORES = 4, 4, 2, 8, 2
WIDE = 8

ITERS = 4


def from_everyone(x, axis):
    devices = lax.axis_size(axis)
    return lax.all_to_all(jnp.broadcast_to(x[None], (devices, *x.shape)), axis, 0, 0, tiled=True)


def joined_along(pieces, dim):
    shape = list(pieces.shape[1:])
    shape[dim] *= pieces.shape[0]
    return jnp.moveaxis(pieces, 0, dim).reshape(shape)


def collect(x, axis, dim):
    pieces = from_everyone(x, axis)
    return joined_along(pieces, dim)


def place():
    member = lax.axis_index("member")
    space = lax.axis_index("space")
    x = lax.rem(member, X)
    y = lax.div(space, Z * CORES) * Y_LO + lax.div(member, X)
    z = lax.rem(lax.div(space, CORES), Z)
    return x, y, z, lax.rem(space, CORES)


def device_at(x, y, z, core):
    member = lax.rem(y, Y_LO) * X + x
    space = (lax.div(y, Y_LO) * Z + z) * CORES + core
    return {"member": member, "space": space}


def sum_kernel(part, total, got_row, sum_row, got_y, sum_y, got_z, all_y, all_row, send_sems, recv_sems):
    x, y, z, core = place()
    row = x * CORES + core

    def row_peer(step):
        other = lax.rem(row + step, WIDE)
        return other, device_at(lax.div(other, CORES), y, z, lax.rem(other, CORES))

    def y_peer(step):
        other = lax.rem(y + step, WIDE)
        return other, device_at(x, other, z, core)

    def z_peer(step):
        other = lax.rem(z + step, WIDE)
        return other, device_at(x, y, other, core)

    barrier = pltpu.get_barrier_semaphore()
    for peer in (row_peer, y_peer, z_peer):
        for step in range(1, WIDE):
            pl.semaphore_signal(barrier, inc=1, device_id=peer(step)[1], device_id_type=pl.DeviceIdType.MESH)
    pl.semaphore_wait(barrier, 3 * (WIDE - 1))

    def exchange(phase, peer, source, target):
        copies = []
        for step in range(1, WIDE):
            other, device = peer(step)
            copy = pltpu.make_async_remote_copy(
                src_ref=source(other),
                dst_ref=target(step),
                send_sem=send_sems.at[phase, step - 1],
                recv_sem=recv_sems.at[phase, step - 1],
                device_id=device,
                device_id_type=pl.DeviceIdType.MESH,
            )
            copy.start()
            copies.append(copy)
        return copies

    def arrived(copies):
        for copy in copies:
            copy.wait_recv()

    sent = []
    copies = exchange(0, row_peer, lambda o: part.at[pl.ds(o * WIDE, WIDE)], lambda s: got_row.at[s - 1])
    sent += copies
    arrived(copies)
    sum_row[...] = part[pl.ds(row * WIDE, WIDE)] + jnp.sum(got_row[...], axis=0)

    copies = exchange(1, y_peer, lambda o: sum_row.at[o], lambda s: got_y.at[s - 1])
    sent += copies
    arrived(copies)
    sum_y[...] = sum_row[y] + jnp.sum(got_y[...], axis=0)

    got_z[z] = sum_y[...]
    copies = exchange(2, z_peer, lambda o: sum_y, lambda s: got_z.at[z])
    sent += copies
    arrived(copies)
    sum_y_z = jnp.sum(got_z[...], axis=0)
    all_y[y] = sum_y_z

    copies = exchange(3, y_peer, lambda o: all_y.at[y], lambda s: all_y.at[y])
    sent += copies
    arrived(copies)

    copies = exchange(4, row_peer, lambda o: all_y, lambda s: all_row.at[row])
    sent += copies
    all_row[row] = all_y[...]
    arrived(copies)
    total[...] = all_row[...].reshape(total.shape)
    for copy in sent:
        copy.wait_send()


def sum_everywhere(part):
    dims = part.shape[1:]
    return pl.pallas_call(
        sum_kernel,
        out_shape=jax.ShapeDtypeStruct(part.shape, jnp.float32),
        in_specs=[pl.BlockSpec(memory_space=pltpu.VMEM)],
        out_specs=pl.BlockSpec(memory_space=pltpu.VMEM),
        scratch_shapes=[
            pltpu.VMEM((WIDE - 1, WIDE, *dims), jnp.float32),
            pltpu.VMEM((WIDE, *dims), jnp.float32),
            pltpu.VMEM((WIDE - 1, *dims), jnp.float32),
            pltpu.VMEM(dims, jnp.float32),
            pltpu.VMEM((WIDE, *dims), jnp.float32),
            pltpu.VMEM((WIDE, *dims), jnp.float32),
            pltpu.VMEM((WIDE, WIDE, *dims), jnp.float32),
            pltpu.SemaphoreType.DMA((5, WIDE - 1)),
            pltpu.SemaphoreType.DMA((5, WIDE - 1)),
        ],
        compiler_params=pltpu.CompilerParams(collective_id=1, has_side_effects=True),
        name="sum_everywhere",
    )(part)


def harmonic(first_cond, second_cond):
    return 2.0 * first_cond * second_cond / (first_cond + second_cond)


HALF = 32
TEAM = 16
COND, SOURCE = ITERS - 1, ITERS


def conjugate_kernel(
    field,
    source,
    wanted,
    picked,
    cond,
    face_x,
    face_y,
    face_z,
    lower_z,
    searched,
    image,
    residual,
    direction,
    along,
    beyond,
    answer,
    cond_edge,
    source_edge,
    edges,
    tiles,
    edge_send,
    edge_recv,
    tile_send,
    tile_recv,
):
    member = lax.axis_index("member")
    plane = (8, 128)
    sublane = lax.broadcasted_iota(jnp.int32, plane, 0)
    lane = lax.broadcasted_iota(jnp.int32, plane, 1)
    lane_4 = lax.broadcasted_iota(jnp.int32, (4, 8, 128), 2)
    low_half = sublane < 4

    def team_peer(step):
        return {"member": lax.rem(member + step, TEAM)}

    def edge_copy(kind, upward):
        if kind == COND:
            origin, target = field.at[3 * upward], cond_edge.at[1 - upward]
        elif kind == SOURCE:
            origin, target = source.at[3 * upward], source_edge.at[1 - upward]
        else:
            origin, target = searched.at[3 * upward, pl.ds(1, HALF)], edges.at[kind, 1 - upward]
        return pltpu.make_async_remote_copy(
            src_ref=origin,
            dst_ref=target,
            send_sem=edge_send.at[kind, upward],
            recv_sem=edge_recv.at[kind, 1 - upward],
            device_id=team_peer(1 if upward else TEAM - 1),
            device_id_type=pl.DeviceIdType.MESH,
        )

    def send_edges(kind):
        @pl.when(member > 0)
        def _():
            edge_copy(kind, 0).start()

        @pl.when(member < TEAM - 1)
        def _():
            edge_copy(kind, 1).start()

    def edges_sent(kind):
        @pl.when(member > 0)
        def _():
            edge_copy(kind, 0).wait_send()

        @pl.when(member < TEAM - 1)
        def _():
            edge_copy(kind, 1).wait_send()

    def edges_here(kind):
        @pl.when(member > 0)
        def _():
            edge_copy(kind, 1).wait_recv()

        @pl.when(member < TEAM - 1)
        def _():
            edge_copy(kind, 0).wait_recv()

    def tile_copy(turn, step):
        return pltpu.make_async_remote_copy(
            src_ref=tiles.at[turn, member],
            dst_ref=tiles.at[turn, member],
            send_sem=tile_send.at[turn, step - 1],
            recv_sem=tile_recv.at[turn, step - 1],
            device_id=team_peer(step),
            device_id_type=pl.DeviceIdType.MESH,
        )

    def send_sums(turn, norm, product):
        norm = norm + pltpu.roll(norm, 64, 1)
        product = product + pltpu.roll(product, 64, 1)
        tiles[turn, member] = jnp.where(lane < 64, norm, product)
        for step in range(1, TEAM):
            tile_copy(turn, step).start()

    def sums_here(turn):
        for step in range(1, TEAM):
            tile_copy(turn, step).wait_recv()
        both = jnp.sum(tiles[turn], axis=0)
        both = both + pltpu.roll(both, 4, 0)
        norm = jnp.sum(jnp.where(lane < 64, both, 0.0), axis=1, keepdims=True)
        product = jnp.sum(jnp.where(lane < 64, 0.0, both), axis=1, keepdims=True)
        return jnp.broadcast_to(norm, plane), jnp.broadcast_to(product, plane)

    def over_rows(body, start, width=2):
        def several(block, carry):
            for k in range(width):
                carry = body(block * width + k, carry)
            return carry

        return lax.fori_loop(0, HALF // width, several, start)

    barrier = pltpu.get_barrier_semaphore()
    for step in range(1, TEAM):
        pl.semaphore_signal(barrier, inc=1, device_id=team_peer(step), device_id_type=pl.DeviceIdType.MESH)
    pl.semaphore_wait(barrier, TEAM - 1)
    send_edges(COND)
    send_edges(SOURCE)

    @pl.when(member == 0)
    def _():
        cond_edge[0] = field[0]
        source_edge[0] = jnp.zeros(source_edge.shape[1:], jnp.float32)
        for kind in range(ITERS - 1):
            edges[kind, 0] = jnp.zeros(edges.shape[2:], jnp.float32)

    @pl.when(member == TEAM - 1)
    def _():
        cond_edge[1] = field[3]
        source_edge[1] = jnp.zeros(source_edge.shape[1:], jnp.float32)
        for kind in range(ITERS - 1):
            edges[kind, 1] = jnp.zeros(edges.shape[2:], jnp.float32)

    def spread_source(rows):
        lower, upper = rows[..., 0:1, :], rows[..., 1:2, :]
        shape = (*rows.shape[:-2], *plane)
        return jnp.where(low_half, jnp.broadcast_to(lower, shape), jnp.broadcast_to(upper, shape))

    def close_ends(padded, outside):
        for y in range(4):
            first, last = padded[y, 1], padded[y, HALF]
            below = first if outside is None else outside
            above = last if outside is None else outside
            padded[y, 0] = jnp.where(low_half, below, pltpu.roll(last, 4, 0))
            padded[y, HALF + 1] = jnp.where(low_half, pltpu.roll(first, 4, 0), above)

    def begin(row, carry):
        cond[:, row + 1] = jnp.exp(field[:, row])
        searched[:, row + 1] = spread_source(source[:, row])
        return carry

    over_rows(begin, 0)
    close_ends(cond, None)
    close_ends(searched, jnp.zeros(plane, jnp.float32))

    def inner_faces(row, carry):
        here = cond[:, row + 1]
        face_x[:, row + 1] = harmonic(here, cond[:, row + 2])
        above = jnp.where(lane_4 == 127, here, pltpu.roll(here, 127, 2))
        upper = harmonic(here, above)
        face_z[:, row] = upper
        lower_z[:, row] = jnp.where(lane_4 == 0, here, pltpu.roll(upper, 1, 2))
        face_y[1:4, row] = harmonic(here[:3], here[1:])
        return carry

    over_rows(inner_faces, 0)
    for y in range(4):
        face_x[y, 0] = harmonic(cond[y, 0], cond[y, 1])
    edges_here(COND)

    def outer_faces(row, carry):
        face_y[0, row] = harmonic(jnp.exp(cond_edge[0, row]), cond[0, row + 1])
        face_y[4, row] = harmonic(cond[3, row + 1], jnp.exp(cond_edge[1, row]))
        return carry

    over_rows(outer_faces, 0)

    def operate(lower_edge, upper_edge):
        def body(row, carry):
            here = searched[:, row + 1]
            before = jnp.concatenate([lower_edge(row)[None], here[:3]])
            after = jnp.concatenate([here[1:], upper_edge(row)[None]])
            result = face_x[:, row + 1] * (here - searched[:, row + 2])
            result = result + face_x[:, row] * (here - searched[:, row])
            result = result + face_y[1:5, row] * (here - after)
            result = result + face_y[0:4, row] * (here - before)
            above = jnp.where(lane_4 == 127, 0.0, pltpu.roll(here, 127, 2))
            below = jnp.where(lane_4 == 0, 0.0, pltpu.roll(here, 1, 2))
            result = result + face_z[:, row] * (here - above)
            image[:, row] = result + lower_z[:, row] * (here - below)
            return carry

        over_rows(body, 0)

    zeros = jnp.zeros(plane, jnp.float32)
    edges_here(SOURCE)
    operate(lambda row: spread_source(source_edge[0, row]), lambda row: spread_source(source_edge[1, row]))

    def first_sums(row, carry):
        norm, product = carry
        image_here = image[:, row]
        residual_here = searched[:, row + 1]
        residual[:, row] = residual_here
        searched[:, row + 1] = image_here
        return norm + jnp.sum(residual_here * residual_here, axis=0), product + jnp.sum(
            residual_here * image_here, axis=0
        )

    norm, product = over_rows(first_sums, (zeros, zeros))

    norm_before = step_before = None
    for turn in range(ITERS):
        last = turn == ITERS - 1
        send_sums(turn, norm, product)
        if not last:
            send_edges(turn)
            close_ends(searched, zeros)
            edges_here(turn)
            operate(lambda row: edges[turn, 0, row], lambda row: edges[turn, 1, row])
        norm_now, product_now = sums_here(turn)
        if turn == 0:
            step_size = norm_now / product_now
        else:
            ratio = norm_now / norm_before
            step_size = norm_now / (product_now - ratio * norm_now / step_before)
        norm_before, step_before = norm_now, step_size

        def update(row, carry):
            norm, product = carry
            residual_here, image_here = residual[:, row], searched[:, row + 1]
            direction_here, along_here, beyond_here = residual_here, image_here, image[:, row]
            answer_here = step_size * direction_here
            if turn > 0:
                direction_here = direction_here + ratio * direction[:, row]
                along_here = along_here + ratio * along[:, row]
                beyond_here = beyond_here + ratio * beyond[:, row]
                answer_here = answer[:, row] + step_size * direction_here
            residual_here = residual_here - step_size * along_here
            image_here = image_here - step_size * beyond_here
            answer[:, row] = answer_here
            direction[:, row] = direction_here
            along[:, row] = along_here
            beyond[:, row] = beyond_here
            residual[:, row] = residual_here
            searched[:, row + 1] = image_here
            return norm + jnp.sum(residual_here * residual_here, axis=0), product + jnp.sum(
                residual_here * image_here, axis=0
            )

        def finish(row, carry):
            answer[:, row] = answer[:, row] + step_size * (residual[:, row] + ratio * direction[:, row])
            return carry

        if last:
            over_rows(finish, 0)
        else:
            edges_sent(turn)
            norm, product = over_rows(update, (zeros, zeros))

    for block in range(HALF // 2):
        chosen = wanted[block]
        value = zeros
        for choice in range(8):
            value = value + jnp.where(chosen == choice, answer[choice % 4, 2 * block + choice // 4], 0.0)
        picked[block] = value[:4]
        picked[HALF // 2 + block] = value[4:]

    edges_sent(COND)
    edges_sent(SOURCE)
    for turn in range(ITERS):
        for step in range(1, TEAM):
            tile_copy(turn, step).wait_send()


def observed_pressure(field, source, wanted):
    held = field.shape
    padded = (held[0], held[1] + 2, *held[2:])
    edge = held[1:]
    vmem = lambda *shape: pltpu.VMEM(shape, jnp.float32)
    return pl.pallas_call(
        conjugate_kernel,
        out_shape=jax.ShapeDtypeStruct((HALF, 4, 128), jnp.float32),
        in_specs=[pl.BlockSpec(memory_space=pltpu.VMEM)] * 3,
        out_specs=pl.BlockSpec(memory_space=pltpu.VMEM),
        scratch_shapes=[
            vmem(*padded),
            vmem(held[0], held[1] + 1, *held[2:]),
            vmem(held[0] + 1, *held[1:]),
            vmem(*held),
            vmem(*held),
            vmem(*padded),
            *[vmem(*held)] * 6,
            vmem(2, *edge),
            vmem(2, *source.shape[1:]),
            vmem(ITERS - 1, 2, *edge),
            vmem(ITERS, TEAM, *held[2:]),
            pltpu.SemaphoreType.DMA((ITERS + 1, 2)),
            pltpu.SemaphoreType.DMA((ITERS + 1, 2)),
            pltpu.SemaphoreType.DMA((ITERS, TEAM - 1)),
            pltpu.SemaphoreType.DMA((ITERS, TEAM - 1)),
        ],
        compiler_params=pltpu.CompilerParams(collective_id=2, has_side_effects=True),
        name="observed_pressure",
    )(field, source, wanted)


def local(ensemble, source, obs_rows, obs_values, obs_noise, obs_var):
    total_members = ensemble.shape[0]
    block_x, block_y, layers = source.shape
    held_fields = lax.all_to_all(ensemble, "space", split_axis=0, concat_axis=1, tiled=True)
    held_count = held_fields.shape[0]
    field = held_fields.reshape(held_count, 2, HALF, block_y, layers).transpose(3, 2, 1, 0, 4)
    field = field.reshape(block_y, HALF, 2 * held_count, layers)
    forcing = collect(source, "space", 0).reshape(2, HALF, block_y, layers).transpose(2, 1, 0, 3)
    gathered_rows = collect(obs_rows, "space", 0).reshape(2, -1).T
    wanted = jnp.broadcast_to(gathered_rows[:, :, None, None], (HALF // 2, 2, held_count, layers))
    picked = observed_pressure(field, forcing, wanted.reshape(HALF // 2, 2 * held_count, layers))
    returned = lax.all_to_all(picked, "space", split_axis=0, concat_axis=0, tiled=True)
    predicted = returned.reshape(total_members, 1, 1, -1)
    flat_pred = returned.reshape(total_members, -1)
    inv_sigma = 1.0 / jnp.sqrt(obs_var.reshape(-1))
    spread = (flat_pred - jnp.mean(flat_pred, axis=0)) * inv_sigma
    misfit = (obs_values.reshape(-1) - flat_pred) * inv_sigma + obs_noise.reshape(total_members, -1)
    gram_part = jnp.dot(spread, spread.T, precision=lax.Precision.HIGHEST)
    cross_part = jnp.dot(spread, misfit.T, precision=lax.Precision.HIGHEST)
    both = sum_everywhere(jnp.concatenate([gram_part, cross_part]).reshape(64, 4, -1))
    gram_sum, cross_sum = jnp.split(both.reshape(2 * total_members, total_members), 2)
    factor = jnp.linalg.cholesky(
        gram_sum + (total_members - 1.0) * jnp.eye(total_members, dtype=jnp.float32)
    )
    weights = jax.scipy.linalg.cho_solve((factor, True), cross_sum)
    flat_field = ensemble.reshape(total_members, -1)
    anomalies = flat_field - jnp.mean(flat_field, axis=0)
    updated = flat_field + jnp.dot(weights.T, anomalies, precision=lax.Precision.HIGHEST)
    return (updated.reshape(ensemble.shape), predicted)


def solution(mesh):
    in_specs = (
        P(None, "space", "member", None),
        P("space", "member", None),
        P("space", "member", None),
        P("space", "member", None),
        P(None, "space", "member", None),
        P("space", "member", None),
    )
    out_specs = (P(None, "space", "member", None), P(None, "space", "member", None))
    return jax.shard_map(local, mesh=mesh, in_specs=in_specs, out_specs=out_specs, check_vma=False)
```

```python
import jax
import jax.numpy as jnp
from jax import lax
from jax.experimental import pallas as pl
from jax.experimental.pallas import tpu as pltpu
from jax.sharding import PartitionSpec as P

X, Y_LO, Y_HI, Z, CORES = 4, 4, 2, 8, 2
WIDE = 8

ITERS = 4


def place():
    member = lax.axis_index("member")
    space = lax.axis_index("space")
    x = lax.rem(member, X)
    y = lax.div(space, Z * CORES) * Y_LO + lax.div(member, X)
    z = lax.rem(lax.div(space, CORES), Z)
    return x, y, z, lax.rem(space, CORES)


def device_at(x, y, z, core):
    member = lax.rem(y, Y_LO) * X + x
    space = (lax.div(y, Y_LO) * Z + z) * CORES + core
    return {"member": member, "space": space}


def sum_kernel(part, total, got_row, sum_row, got_y, sum_y, got_z, all_y, all_row, send_sems, recv_sems):
    x, y, z, core = place()
    row = x * CORES + core

    def row_peer(step):
        other = lax.rem(row + step, WIDE)
        return other, device_at(lax.div(other, CORES), y, z, lax.rem(other, CORES))

    def y_peer(step):
        other = lax.rem(y + step, WIDE)
        return other, device_at(x, other, z, core)

    def z_peer(step):
        other = lax.rem(z + step, WIDE)
        return other, device_at(x, y, other, core)

    barrier = pltpu.get_barrier_semaphore()
    for peer in (row_peer, y_peer, z_peer):
        for step in range(1, WIDE):
            pl.semaphore_signal(barrier, inc=1, device_id=peer(step)[1], device_id_type=pl.DeviceIdType.MESH)
    pl.semaphore_wait(barrier, 3 * (WIDE - 1))

    def exchange(phase, peer, source, target):
        copies = []
        for step in range(1, WIDE):
            other, device = peer(step)
            copy = pltpu.make_async_remote_copy(
                src_ref=source(other),
                dst_ref=target(step),
                send_sem=send_sems.at[phase, step - 1],
                recv_sem=recv_sems.at[phase, step - 1],
                device_id=device,
                device_id_type=pl.DeviceIdType.MESH,
            )
            copy.start()
            copies.append(copy)
        return copies

    def arrived(copies):
        for copy in copies:
            copy.wait_recv()

    sent = []
    copies = exchange(0, row_peer, lambda o: part.at[pl.ds(o * WIDE, WIDE)], lambda s: got_row.at[s - 1])
    sent += copies
    arrived(copies)
    sum_row[...] = part[pl.ds(row * WIDE, WIDE)] + jnp.sum(got_row[...], axis=0)

    copies = exchange(1, y_peer, lambda o: sum_row.at[o], lambda s: got_y.at[s - 1])
    sent += copies
    arrived(copies)
    sum_y[...] = sum_row[y] + jnp.sum(got_y[...], axis=0)

    got_z[z] = sum_y[...]
    copies = exchange(2, z_peer, lambda o: sum_y, lambda s: got_z.at[z])
    sent += copies
    arrived(copies)
    sum_y_z = jnp.sum(got_z[...], axis=0)
    all_y[y] = sum_y_z

    copies = exchange(3, y_peer, lambda o: all_y.at[y], lambda s: all_y.at[y])
    sent += copies
    arrived(copies)

    copies = exchange(4, row_peer, lambda o: all_y, lambda s: all_row.at[row])
    sent += copies
    all_row[row] = all_y[...]
    arrived(copies)
    total[...] = all_row[...].reshape(total.shape)
    for copy in sent:
        copy.wait_send()


def sum_everywhere(part):
    dims = part.shape[1:]
    return pl.pallas_call(
        sum_kernel,
        out_shape=jax.ShapeDtypeStruct(part.shape, jnp.float32),
        in_specs=[pl.BlockSpec(memory_space=pltpu.VMEM)],
        out_specs=pl.BlockSpec(memory_space=pltpu.VMEM),
        scratch_shapes=[
            pltpu.VMEM((WIDE - 1, WIDE, *dims), jnp.float32),
            pltpu.VMEM((WIDE, *dims), jnp.float32),
            pltpu.VMEM((WIDE - 1, *dims), jnp.float32),
            pltpu.VMEM(dims, jnp.float32),
            pltpu.VMEM((WIDE, *dims), jnp.float32),
            pltpu.VMEM((WIDE, *dims), jnp.float32),
            pltpu.VMEM((WIDE, WIDE, *dims), jnp.float32),
            pltpu.SemaphoreType.DMA((5, WIDE - 1)),
            pltpu.SemaphoreType.DMA((5, WIDE - 1)),
        ],
        compiler_params=pltpu.CompilerParams(collective_id=1, has_side_effects=True),
        name="sum_everywhere",
    )(part)


def harmonic(first_cond, second_cond):
    return 2.0 * first_cond * second_cond / (first_cond + second_cond)


HALF = 32
TEAM = 16
SPACE = 32
COND, SOURCE = ITERS - 1, ITERS


def conjugate_kernel(
    ensemble,
    source,
    wanted,
    predicted,
    held_rows,
    held_source,
    held_wanted,
    picked,
    returned,
    side,
    cond,
    face_x,
    face_y,
    face_z,
    lower_z,
    searched,
    image,
    residual,
    direction,
    along,
    beyond,
    answer,
    cond_edge,
    source_edge,
    edges,
    tiles,
    edge_send,
    edge_recv,
    tile_send,
    tile_recv,
    swap_send,
    swap_recv,
    own_sems,
):
    member = lax.axis_index("member")
    space = lax.axis_index("space")
    plane = (8, 128)
    sublane = lax.broadcasted_iota(jnp.int32, plane, 0)
    lane = lax.broadcasted_iota(jnp.int32, plane, 1)
    lane_4 = lax.broadcasted_iota(jnp.int32, (4, 8, 128), 2)
    low_half = sublane < 4

    def team_peer(step):
        return {"member": lax.rem(member + step, TEAM)}

    def edge_copy(kind, upward):
        if kind == COND:
            origin, target = cond.at[3 * upward, pl.ds(1, HALF)], cond_edge.at[1 - upward]
        elif kind == SOURCE:
            origin, target = side.at[upward], source_edge.at[1 - upward]
        else:
            origin, target = searched.at[3 * upward, pl.ds(1, HALF)], edges.at[kind, 1 - upward]
        return pltpu.make_async_remote_copy(
            src_ref=origin,
            dst_ref=target,
            send_sem=edge_send.at[kind, upward],
            recv_sem=edge_recv.at[kind, 1 - upward],
            device_id=team_peer(1 if upward else TEAM - 1),
            device_id_type=pl.DeviceIdType.MESH,
        )

    def send_edges(kind):
        @pl.when(member > 0)
        def _():
            edge_copy(kind, 0).start()

        @pl.when(member < TEAM - 1)
        def _():
            edge_copy(kind, 1).start()

    def edges_sent(kind):
        @pl.when(member > 0)
        def _():
            edge_copy(kind, 0).wait_send()

        @pl.when(member < TEAM - 1)
        def _():
            edge_copy(kind, 1).wait_send()

    def edges_here(kind):
        @pl.when(member > 0)
        def _():
            edge_copy(kind, 1).wait_recv()

        @pl.when(member < TEAM - 1)
        def _():
            edge_copy(kind, 0).wait_recv()

    def tile_copy(turn, step):
        return pltpu.make_async_remote_copy(
            src_ref=tiles.at[turn, member],
            dst_ref=tiles.at[turn, member],
            send_sem=tile_send.at[turn],
            recv_sem=tile_recv.at[turn],
            device_id=team_peer(step),
            device_id_type=pl.DeviceIdType.MESH,
        )

    def wait_bytes(ref, sem):
        pltpu.make_async_copy(ref, ref, sem).wait()

    def space_peer(step):
        other = lax.rem(space + step, SPACE)
        return other, {"space": other}

    def halves(index):
        return lax.rem(index, HALF // 2), lax.div(index, HALF // 2)

    def piece_refs(other):
        block, half = halves(space)
        rows = pl.ds(pl.multiple_of(half * 32, 32), 32)
        return (
            (ensemble.at[pl.ds(pl.multiple_of(other * 32, 32), 32)], held_rows.at[block, rows]),
            (source, held_source.at[block, pl.ds(pl.multiple_of(half * 8, 8), 8)]),
            (wanted, held_wanted.at[space]),
        )

    def swap(step):
        other, device = space_peer(step)
        for kind, (origin, target) in enumerate(piece_refs(other)):
            pltpu.make_async_remote_copy(
                src_ref=origin,
                dst_ref=target,
                send_sem=swap_send.at[kind],
                recv_sem=swap_recv.at[kind],
                device_id=device,
                device_id_type=pl.DeviceIdType.MESH,
            ).start()

    def send_sums(turn, norm, product):
        norm = norm + pltpu.roll(norm, 64, 1)
        product = product + pltpu.roll(product, 64, 1)
        tiles[turn, member] = jnp.where(lane < 64, norm, product)
        for step in range(1, TEAM):
            tile_copy(turn, step).start()

    def sums_here(turn):
        wait_bytes(tiles.at[turn, pl.ds(0, TEAM - 1)], tile_recv.at[turn])
        both = jnp.sum(tiles[turn], axis=0)
        both = both + pltpu.roll(both, 4, 0)
        norm = jnp.sum(jnp.where(lane < 64, both, 0.0), axis=1, keepdims=True)
        product = jnp.sum(jnp.where(lane < 64, 0.0, both), axis=1, keepdims=True)
        return jnp.broadcast_to(norm, plane), jnp.broadcast_to(product, plane)

    def over_rows(body, start):
        def several(block, carry):
            for k in range(2):
                carry = body(block, k, carry)
            return carry

        return lax.fori_loop(0, HALF // 2, several, start)

    barrier = pltpu.get_barrier_semaphore()
    for step in range(1, SPACE):
        pl.semaphore_signal(barrier, inc=1, device_id=space_peer(step)[1], device_id_type=pl.DeviceIdType.MESH)
    for step in range(1, TEAM):
        pl.semaphore_signal(barrier, inc=1, device_id=team_peer(step), device_id_type=pl.DeviceIdType.MESH)
    own = [
        pltpu.make_async_copy(origin, target, own_sems.at[kind])
        for kind, (origin, target) in enumerate(piece_refs(space))
    ]
    for copy in own:
        copy.start()
    pl.semaphore_wait(barrier, TEAM + SPACE - 2)
    for step in range(1, SPACE):
        swap(step)

    @pl.when(member == 0)
    def _():
        source_edge[0] = jnp.zeros(source_edge.shape[1:], jnp.float32)
        for kind in range(ITERS - 1):
            edges[kind, 0] = jnp.zeros(edges.shape[2:], jnp.float32)

    @pl.when(member == TEAM - 1)
    def _():
        source_edge[1] = jnp.zeros(source_edge.shape[1:], jnp.float32)
        for kind in range(ITERS - 1):
            edges[kind, 1] = jnp.zeros(edges.shape[2:], jnp.float32)

    for copy in own:
        copy.wait()
    others = SPACE - 1
    wait_bytes(ensemble.at[pl.ds(0, others * 32)], swap_recv.at[0])
    wait_bytes(ensemble.at[pl.ds(0, others * 8)], swap_recv.at[1])
    wait_bytes(held_wanted.at[pl.ds(0, others)], swap_recv.at[2])

    def two_rows(lower, upper):
        return jnp.where(low_half, jnp.broadcast_to(lower, plane), jnp.broadcast_to(upper, plane))

    def close_ends(padded, outside):
        for y in range(4):
            first, last = padded[y, 1], padded[y, HALF]
            below = first if outside is None else outside
            above = last if outside is None else outside
            padded[y, 0] = jnp.where(low_half, below, pltpu.roll(last, 4, 0))
            padded[y, HALF + 1] = jnp.where(low_half, pltpu.roll(first, 4, 0), above)

    def begin(block, carry):
        rows = held_source[block]
        for k in range(2):
            for y in range(4):
                at = 4 * k + y
                held = held_rows[block, pl.ds(at, 8, stride=8), :]
                cond[y, 2 * block + k + 1] = jnp.exp(held)
                searched[y, 2 * block + k + 1] = two_rows(rows[at : at + 1], rows[8 + at : 9 + at])
        for upward in range(2):
            at = 3 * upward
            side[upward, block] = jnp.concatenate([rows[at + k : at + k + 1] for k in (0, 8, 4, 12)])
        return carry

    lax.fori_loop(0, HALF // 2, begin, 0)
    send_edges(COND)
    send_edges(SOURCE)
    close_ends(cond, None)
    close_ends(searched, jnp.zeros(plane, jnp.float32))

    @pl.when(member == 0)
    def _():
        cond_edge[0] = cond[0, pl.ds(1, HALF)]

    @pl.when(member == TEAM - 1)
    def _():
        cond_edge[1] = cond[3, pl.ds(1, HALF)]

    def inner_faces(block, k, carry):
        row = 2 * block + k
        here = cond[:, row + 1]
        face_x[:, row + 1] = harmonic(here, cond[:, row + 2])
        above = jnp.where(lane_4 == 127, here, pltpu.roll(here, 127, 2))
        upper = harmonic(here, above)
        face_z[:, row] = upper
        lower_z[:, row] = jnp.where(lane_4 == 0, here, pltpu.roll(upper, 1, 2))
        face_y[1:4, row] = harmonic(here[:3], here[1:])
        return carry

    over_rows(inner_faces, 0)
    for y in range(4):
        face_x[y, 0] = harmonic(cond[y, 0], cond[y, 1])
    edges_here(COND)

    def outer_faces(block, k, carry):
        row = 2 * block + k
        face_y[0, row] = harmonic(cond_edge[0, row], cond[0, row + 1])
        face_y[4, row] = harmonic(cond[3, row + 1], cond_edge[1, row])
        return carry

    over_rows(outer_faces, 0)

    def operate(lower_edge, upper_edge):
        def body(block, k, carry):
            row = 2 * block + k
            here = searched[:, row + 1]
            before = jnp.concatenate([lower_edge(block, k)[None], here[:3]])
            after = jnp.concatenate([here[1:], upper_edge(block, k)[None]])
            result = face_x[:, row + 1] * (here - searched[:, row + 2])
            result = result + face_x[:, row] * (here - searched[:, row])
            result = result + face_y[1:5, row] * (here - after)
            result = result + face_y[0:4, row] * (here - before)
            above = jnp.where(lane_4 == 127, 0.0, pltpu.roll(here, 127, 2))
            below = jnp.where(lane_4 == 0, 0.0, pltpu.roll(here, 1, 2))
            result = result + face_z[:, row] * (here - above)
            image[:, row] = result + lower_z[:, row] * (here - below)
            return carry

        over_rows(body, 0)

    zeros = jnp.zeros(plane, jnp.float32)
    edges_here(SOURCE)

    def source_side(upward):
        def rows(block, k):
            four = source_edge[upward, block]
            return two_rows(four[2 * k : 2 * k + 1], four[2 * k + 1 : 2 * k + 2])

        return rows

    operate(source_side(0), source_side(1))

    def first_sums(block, k, carry):
        row = 2 * block + k
        norm, product = carry
        image_here = image[:, row]
        residual_here = searched[:, row + 1]
        residual[:, row] = residual_here
        searched[:, row + 1] = image_here
        return norm + jnp.sum(residual_here * residual_here, axis=0), product + jnp.sum(
            residual_here * image_here, axis=0
        )

    norm, product = over_rows(first_sums, (zeros, zeros))

    norm_before = step_before = None
    for turn in range(ITERS):
        last = turn == ITERS - 1
        send_sums(turn, norm, product)
        if not last:
            send_edges(turn)
            close_ends(searched, zeros)
            edges_here(turn)
            operate(lambda block, k: edges[turn, 0, 2 * block + k], lambda block, k: edges[turn, 1, 2 * block + k])
        norm_now, product_now = sums_here(turn)
        if turn == 0:
            step_size = norm_now / product_now
        else:
            ratio = norm_now / norm_before
            step_size = norm_now / (product_now - ratio * norm_now / step_before)
        norm_before, step_before = norm_now, step_size

        def update(block, k, carry):
            row = 2 * block + k
            norm, product = carry
            residual_here, image_here = residual[:, row], searched[:, row + 1]
            direction_here, along_here, beyond_here = residual_here, image_here, image[:, row]
            answer_here = step_size * direction_here
            if turn > 0:
                direction_here = direction_here + ratio * direction[:, row]
                along_here = along_here + ratio * along[:, row]
                beyond_here = beyond_here + ratio * beyond[:, row]
                answer_here = answer[:, row] + step_size * direction_here
            residual_here = residual_here - step_size * along_here
            image_here = image_here - step_size * beyond_here
            answer[:, row] = answer_here
            direction[:, row] = direction_here
            along[:, row] = along_here
            beyond[:, row] = beyond_here
            residual[:, row] = residual_here
            searched[:, row + 1] = image_here
            return norm + jnp.sum(residual_here * residual_here, axis=0), product + jnp.sum(
                residual_here * image_here, axis=0
            )

        def finish(block, k, carry):
            row = 2 * block + k
            answer[:, row] = answer[:, row] + step_size * (residual[:, row] + ratio * direction[:, row])
            return carry

        if last:
            over_rows(finish, 0)
        else:
            edges_sent(turn)
            norm, product = over_rows(update, (zeros, zeros))

    for block in range(HALF // 2):
        chosen = two_rows(held_wanted[block], held_wanted[HALF // 2 + block])
        value = zeros
        for choice in range(8):
            value = value + jnp.where(chosen == choice, answer[choice % 4, 2 * block + choice // 4], 0.0)
        picked[block] = value[:4]
        picked[HALF // 2 + block] = value[4:]

    returned[space] = picked[space]
    for step in range(1, SPACE):
        other, device = space_peer(step)
        pltpu.make_async_remote_copy(
            src_ref=picked.at[other],
            dst_ref=returned.at[space],
            send_sem=swap_send.at[3],
            recv_sem=swap_recv.at[3],
            device_id=device,
            device_id_type=pl.DeviceIdType.MESH,
        ).start()
    wait_bytes(returned.at[pl.ds(0, others)], swap_recv.at[3])
    predicted[...] = returned[...]

    edges_sent(COND)
    edges_sent(SOURCE)
    for turn in range(ITERS):
        wait_bytes(tiles.at[turn, pl.ds(0, TEAM - 1)], tile_send.at[turn])
    wait_bytes(ensemble.at[pl.ds(0, others * 32)], swap_send.at[0])
    wait_bytes(ensemble.at[pl.ds(0, others * 8)], swap_send.at[1])
    wait_bytes(held_wanted.at[pl.ds(0, others)], swap_send.at[2])
    wait_bytes(returned.at[pl.ds(0, others)], swap_send.at[3])


def predict(ensemble, source, wanted):
    held = (4, HALF, 8, 128)
    padded = (4, HALF + 2, 8, 128)
    vmem = lambda *shape: pltpu.VMEM(shape, jnp.float32)
    return pl.pallas_call(
        conjugate_kernel,
        out_shape=jax.ShapeDtypeStruct((SPACE, 4, 128), jnp.float32),
        in_specs=[pl.BlockSpec(memory_space=pl.ANY), *[pl.BlockSpec(memory_space=pltpu.VMEM)] * 2],
        out_specs=pl.BlockSpec(memory_space=pltpu.VMEM),
        scratch_shapes=[
            vmem(HALF // 2, 64, 128),
            vmem(HALF // 2, 16, 128),
            pltpu.VMEM((SPACE, 1, 128), jnp.int32),
            vmem(SPACE, 4, 128),
            vmem(SPACE, 4, 128),
            vmem(2, HALF // 2, 4, 128),
            vmem(*padded),
            vmem(4, HALF + 1, 8, 128),
            vmem(5, HALF, 8, 128),
            vmem(*held),
            vmem(*held),
            vmem(*padded),
            *[vmem(*held)] * 6,
            vmem(2, HALF, 8, 128),
            vmem(2, HALF // 2, 4, 128),
            vmem(ITERS - 1, 2, HALF, 8, 128),
            vmem(ITERS, TEAM, 8, 128),
            pltpu.SemaphoreType.DMA((ITERS + 1, 2)),
            pltpu.SemaphoreType.DMA((ITERS + 1, 2)),
            pltpu.SemaphoreType.DMA((ITERS,)),
            pltpu.SemaphoreType.DMA((ITERS,)),
            pltpu.SemaphoreType.DMA((4,)),
            pltpu.SemaphoreType.DMA((4,)),
            pltpu.SemaphoreType.DMA((3,)),
        ],
        compiler_params=pltpu.CompilerParams(collective_id=2, has_side_effects=True),
        name="predict",
    )(ensemble, source, wanted)


def local(ensemble, source, obs_rows, obs_values, obs_noise, obs_var):
    total_members = ensemble.shape[0]
    layers = source.shape[-1]
    wanted = jnp.broadcast_to(obs_rows.reshape(1, 1), (1, layers))
    returned = predict(ensemble.reshape(-1, layers), source.reshape(-1, layers), wanted)
    predicted = returned.reshape(total_members, 1, 1, -1)
    flat_pred = returned.reshape(total_members, -1)
    inv_sigma = 1.0 / jnp.sqrt(obs_var.reshape(-1))
    spread = (flat_pred - jnp.mean(flat_pred, axis=0)) * inv_sigma
    misfit = (obs_values.reshape(-1) - flat_pred) * inv_sigma + obs_noise.reshape(total_members, -1)
    gram_part = jnp.dot(spread, spread.T, precision=lax.Precision.HIGHEST)
    cross_part = jnp.dot(spread, misfit.T, precision=lax.Precision.HIGHEST)
    both = sum_everywhere(jnp.concatenate([gram_part, cross_part]).reshape(64, 4, -1))
    gram_sum, cross_sum = jnp.split(both.reshape(2 * total_members, total_members), 2)
    factor = jnp.linalg.cholesky(
        gram_sum + (total_members - 1.0) * jnp.eye(total_members, dtype=jnp.float32)
    )
    weights = jax.scipy.linalg.cho_solve((factor, True), cross_sum)
    flat_field = ensemble.reshape(total_members, -1)
    anomalies = flat_field - jnp.mean(flat_field, axis=0)
    updated = flat_field + jnp.dot(weights.T, anomalies, precision=lax.Precision.HIGHEST)
    return (updated.reshape(ensemble.shape), predicted)


def solution(mesh):
    in_specs = (
        P(None, "space", "member", None),
        P("space", "member", None),
        P("space", "member", None),
        P("space", "member", None),
        P(None, "space", "member", None),
        P("space", "member", None),
    )
    out_specs = (P(None, "space", "member", None), P(None, "space", "member", None))
    return jax.shard_map(local, mesh=mesh, in_specs=in_specs, out_specs=out_specs, check_vma=False)
```

```python
import functools

import jax
import jax.numpy as jnp
from jax import lax
from jax.experimental import pallas as pl
from jax.experimental.pallas import tpu as pltpu
from jax.sharding import PartitionSpec as P

X, Y_LO, Y_HI, Z, CORES = 4, 4, 2, 8, 2
WIDE = 8

ITERS = 4


def place():
    member = lax.axis_index("member")
    space = lax.axis_index("space")
    x = lax.rem(member, X)
    y = lax.div(space, Z * CORES) * Y_LO + lax.div(member, X)
    z = lax.rem(lax.div(space, CORES), Z)
    return x, y, z, lax.rem(space, CORES)


def device_at(x, y, z, core):
    member = lax.rem(y, Y_LO) * X + x
    space = (lax.div(y, Y_LO) * Z + z) * CORES + core
    return {"member": member, "space": space}


def sum_peers():
    x, y, z, core = place()
    row = x * CORES + core

    def row_peer(step):
        other = lax.rem(row + step, WIDE)
        return other, device_at(lax.div(other, CORES), y, z, lax.rem(other, CORES))

    def y_peer(step):
        other = lax.rem(y + step, WIDE)
        return other, device_at(x, other, z, core)

    def z_peer(step):
        other = lax.rem(z + step, WIDE)
        return other, device_at(x, y, other, core)

    return (row, y, z), (row_peer, y_peer, z_peer)


def sum_everywhere(part, total, got_row, sum_row, got_y, sum_y, got_z, all_y, all_row, send_sems, recv_sems):
    (row, y, z), (row_peer, y_peer, z_peer) = sum_peers()

    def exchange(phase, peer, source, target):
        copies = []
        for step in range(1, WIDE):
            other, device = peer(step)
            copy = pltpu.make_async_remote_copy(
                src_ref=source(other),
                dst_ref=target(step),
                send_sem=send_sems.at[phase, step - 1],
                recv_sem=recv_sems.at[phase, step - 1],
                device_id=device,
                device_id_type=pl.DeviceIdType.MESH,
            )
            copy.start()
            copies.append(copy)
        return copies

    def arrived(copies):
        for copy in copies:
            copy.wait_recv()

    sent = []
    copies = exchange(0, row_peer, lambda o: part.at[pl.ds(o * WIDE, WIDE)], lambda s: got_row.at[s - 1])
    sent += copies
    arrived(copies)
    sum_row[...] = part[pl.ds(row * WIDE, WIDE)] + jnp.sum(got_row[...], axis=0)

    copies = exchange(1, y_peer, lambda o: sum_row.at[o], lambda s: got_y.at[s - 1])
    sent += copies
    arrived(copies)
    sum_y[...] = sum_row[y] + jnp.sum(got_y[...], axis=0)

    got_z[z] = sum_y[...]
    copies = exchange(2, z_peer, lambda o: sum_y, lambda s: got_z.at[z])
    sent += copies
    arrived(copies)
    sum_y_z = jnp.sum(got_z[...], axis=0)
    all_y[y] = sum_y_z

    copies = exchange(3, y_peer, lambda o: all_y.at[y], lambda s: all_y.at[y])
    sent += copies
    arrived(copies)

    copies = exchange(4, row_peer, lambda o: all_y, lambda s: all_row.at[row])
    sent += copies
    all_row[row] = all_y[...]
    arrived(copies)
    for i in range(WIDE):
        for j in range(0, WIDE, 2):
            total[pl.ds(4 * (WIDE * i + j), 8)] = jnp.concatenate([all_row[i, j], all_row[i, j + 1]])
    for copy in sent:
        copy.wait_send()


def harmonic(first_cond, second_cond):
    return 2.0 * first_cond * second_cond / (first_cond + second_cond)


HALF = 32
TEAM = 16
SPACE = 32
COND, SOURCE = ITERS - 1, ITERS


def conjugate_kernel(
    ensemble,
    source,
    wanted,
    obs_values,
    obs_noise,
    obs_var,
    predicted,
    total,
    held_rows,
    held_source,
    held_wanted,
    picked,
    returned,
    side,
    cond,
    face_x,
    face_y,
    face_z,
    lower_z,
    searched,
    image,
    residual,
    direction,
    along,
    beyond,
    answer,
    cond_edge,
    source_edge,
    edges,
    tiles,
    edge_send,
    edge_recv,
    tile_send,
    tile_recv,
    swap_send,
    swap_recv,
    own_sems,
    part,
    *sum_refs,
):
    member = lax.axis_index("member")
    space = lax.axis_index("space")
    plane = (8, 128)
    sublane = lax.broadcasted_iota(jnp.int32, plane, 0)
    lane = lax.broadcasted_iota(jnp.int32, plane, 1)
    lane_4 = lax.broadcasted_iota(jnp.int32, (4, 8, 128), 2)
    low_half = sublane < 4

    def team_peer(step):
        return {"member": lax.rem(member + step, TEAM)}

    def edge_copy(kind, upward):
        if kind == COND:
            origin, target = cond.at[3 * upward, pl.ds(1, HALF)], cond_edge.at[1 - upward]
        elif kind == SOURCE:
            origin, target = side.at[upward], source_edge.at[1 - upward]
        else:
            origin, target = searched.at[3 * upward, pl.ds(1, HALF)], edges.at[kind, 1 - upward]
        return pltpu.make_async_remote_copy(
            src_ref=origin,
            dst_ref=target,
            send_sem=edge_send.at[kind, upward],
            recv_sem=edge_recv.at[kind, 1 - upward],
            device_id=team_peer(1 if upward else TEAM - 1),
            device_id_type=pl.DeviceIdType.MESH,
        )

    def send_edges(kind):
        @pl.when(member > 0)
        def _():
            edge_copy(kind, 0).start()

        @pl.when(member < TEAM - 1)
        def _():
            edge_copy(kind, 1).start()

    def edges_sent(kind):
        @pl.when(member > 0)
        def _():
            edge_copy(kind, 0).wait_send()

        @pl.when(member < TEAM - 1)
        def _():
            edge_copy(kind, 1).wait_send()

    def edges_here(kind):
        @pl.when(member > 0)
        def _():
            edge_copy(kind, 1).wait_recv()

        @pl.when(member < TEAM - 1)
        def _():
            edge_copy(kind, 0).wait_recv()

    def tile_copy(turn, step):
        return pltpu.make_async_remote_copy(
            src_ref=tiles.at[turn, member],
            dst_ref=tiles.at[turn, member],
            send_sem=tile_send.at[turn],
            recv_sem=tile_recv.at[turn],
            device_id=team_peer(step),
            device_id_type=pl.DeviceIdType.MESH,
        )

    def wait_bytes(ref, sem):
        pltpu.make_async_copy(ref, ref, sem).wait()

    def space_peer(step):
        other = lax.rem(space + step, SPACE)
        return other, {"space": other}

    def halves(index):
        return lax.rem(index, HALF // 2), lax.div(index, HALF // 2)

    def piece_refs(other):
        block, half = halves(space)
        rows = pl.ds(pl.multiple_of(half * 32, 32), 32)
        return (
            (ensemble.at[pl.ds(pl.multiple_of(other * 32, 32), 32)], held_rows.at[block, rows]),
            (source, held_source.at[block, pl.ds(pl.multiple_of(half * 8, 8), 8)]),
            (wanted, held_wanted.at[space]),
        )

    def swap(step):
        other, device = space_peer(step)
        for kind, (origin, target) in enumerate(piece_refs(other)):
            pltpu.make_async_remote_copy(
                src_ref=origin,
                dst_ref=target,
                send_sem=swap_send.at[kind],
                recv_sem=swap_recv.at[kind],
                device_id=device,
                device_id_type=pl.DeviceIdType.MESH,
            ).start()

    def send_sums(turn, norm, product):
        norm = norm + pltpu.roll(norm, 64, 1)
        product = product + pltpu.roll(product, 64, 1)
        tiles[turn, member] = jnp.where(lane < 64, norm, product)
        for step in range(1, TEAM):
            tile_copy(turn, step).start()

    def sums_here(turn):
        wait_bytes(tiles.at[turn, pl.ds(0, TEAM - 1)], tile_recv.at[turn])
        both = jnp.sum(tiles[turn], axis=0)
        both = both + pltpu.roll(both, 4, 0)
        norm = jnp.sum(jnp.where(lane < 64, both, 0.0), axis=1, keepdims=True)
        product = jnp.sum(jnp.where(lane < 64, 0.0, both), axis=1, keepdims=True)
        return jnp.broadcast_to(norm, plane), jnp.broadcast_to(product, plane)

    def over_rows(body, start):
        def several(block, carry):
            for k in range(2):
                carry = body(block, k, carry)
            return carry

        return lax.fori_loop(0, HALF // 2, several, start)

    barrier = pltpu.get_barrier_semaphore()
    for step in range(1, SPACE):
        pl.semaphore_signal(barrier, inc=1, device_id=space_peer(step)[1], device_id_type=pl.DeviceIdType.MESH)
    for step in range(1, TEAM):
        pl.semaphore_signal(barrier, inc=1, device_id=team_peer(step), device_id_type=pl.DeviceIdType.MESH)
    for peer in sum_peers()[1]:
        for step in range(1, WIDE):
            pl.semaphore_signal(barrier, inc=1, device_id=peer(step)[1], device_id_type=pl.DeviceIdType.MESH)
    own = [
        pltpu.make_async_copy(origin, target, own_sems.at[kind])
        for kind, (origin, target) in enumerate(piece_refs(space))
    ]
    for copy in own:
        copy.start()
    pl.semaphore_wait(barrier, TEAM - 1 + SPACE - 1 + 3 * (WIDE - 1))
    for step in range(1, SPACE):
        swap(step)

    @pl.when(member == 0)
    def _():
        source_edge[0] = jnp.zeros(source_edge.shape[1:], jnp.float32)
        for kind in range(ITERS - 1):
            edges[kind, 0] = jnp.zeros(edges.shape[2:], jnp.float32)

    @pl.when(member == TEAM - 1)
    def _():
        source_edge[1] = jnp.zeros(source_edge.shape[1:], jnp.float32)
        for kind in range(ITERS - 1):
            edges[kind, 1] = jnp.zeros(edges.shape[2:], jnp.float32)

    for copy in own:
        copy.wait()
    others = SPACE - 1
    wait_bytes(ensemble.at[pl.ds(0, others * 32)], swap_recv.at[0])
    wait_bytes(ensemble.at[pl.ds(0, others * 8)], swap_recv.at[1])
    wait_bytes(held_wanted.at[pl.ds(0, others)], swap_recv.at[2])

    def two_rows(lower, upper):
        return jnp.where(low_half, jnp.broadcast_to(lower, plane), jnp.broadcast_to(upper, plane))

    def close_ends(padded, outside):
        for y in range(4):
            first, last = padded[y, 1], padded[y, HALF]
            below = first if outside is None else outside
            above = last if outside is None else outside
            padded[y, 0] = jnp.where(low_half, below, pltpu.roll(last, 4, 0))
            padded[y, HALF + 1] = jnp.where(low_half, pltpu.roll(first, 4, 0), above)

    def begin(block, carry):
        rows = held_source[block]
        for k in range(2):
            for y in range(4):
                at = 4 * k + y
                held = held_rows[block, pl.ds(at, 8, stride=8), :]
                cond[y, 2 * block + k + 1] = jnp.exp(held)
                searched[y, 2 * block + k + 1] = two_rows(rows[at : at + 1], rows[8 + at : 9 + at])
        for upward in range(2):
            at = 3 * upward
            side[upward, block] = jnp.concatenate([rows[at + k : at + k + 1] for k in (0, 8, 4, 12)])
        return carry

    lax.fori_loop(0, HALF // 2, begin, 0)
    send_edges(COND)
    send_edges(SOURCE)
    close_ends(cond, None)
    close_ends(searched, jnp.zeros(plane, jnp.float32))

    @pl.when(member == 0)
    def _():
        cond_edge[0] = cond[0, pl.ds(1, HALF)]

    @pl.when(member == TEAM - 1)
    def _():
        cond_edge[1] = cond[3, pl.ds(1, HALF)]

    def inner_faces(block, k, carry):
        row = 2 * block + k
        here = cond[:, row + 1]
        face_x[:, row + 1] = harmonic(here, cond[:, row + 2])
        above = jnp.where(lane_4 == 127, here, pltpu.roll(here, 127, 2))
        upper = harmonic(here, above)
        face_z[:, row] = upper
        lower_z[:, row] = jnp.where(lane_4 == 0, here, pltpu.roll(upper, 1, 2))
        face_y[1:4, row] = harmonic(here[:3], here[1:])
        return carry

    over_rows(inner_faces, 0)
    for y in range(4):
        face_x[y, 0] = harmonic(cond[y, 0], cond[y, 1])
    edges_here(COND)

    def outer_faces(block, k, carry):
        row = 2 * block + k
        face_y[0, row] = harmonic(cond_edge[0, row], cond[0, row + 1])
        face_y[4, row] = harmonic(cond[3, row + 1], cond_edge[1, row])
        return carry

    over_rows(outer_faces, 0)

    def operate(lower_edge, upper_edge):
        def body(block, k, carry):
            row = 2 * block + k
            here = searched[:, row + 1]
            before = jnp.concatenate([lower_edge(block, k)[None], here[:3]])
            after = jnp.concatenate([here[1:], upper_edge(block, k)[None]])
            result = face_x[:, row + 1] * (here - searched[:, row + 2])
            result = result + face_x[:, row] * (here - searched[:, row])
            result = result + face_y[1:5, row] * (here - after)
            result = result + face_y[0:4, row] * (here - before)
            above = jnp.where(lane_4 == 127, 0.0, pltpu.roll(here, 127, 2))
            below = jnp.where(lane_4 == 0, 0.0, pltpu.roll(here, 1, 2))
            result = result + face_z[:, row] * (here - above)
            image[:, row] = result + lower_z[:, row] * (here - below)
            return carry

        over_rows(body, 0)

    zeros = jnp.zeros(plane, jnp.float32)
    edges_here(SOURCE)

    def source_side(upward):
        def rows(block, k):
            four = source_edge[upward, block]
            return two_rows(four[2 * k : 2 * k + 1], four[2 * k + 1 : 2 * k + 2])

        return rows

    operate(source_side(0), source_side(1))

    def first_sums(block, k, carry):
        row = 2 * block + k
        norm, product = carry
        image_here = image[:, row]
        residual_here = searched[:, row + 1]
        residual[:, row] = residual_here
        searched[:, row + 1] = image_here
        return norm + jnp.sum(residual_here * residual_here, axis=0), product + jnp.sum(
            residual_here * image_here, axis=0
        )

    norm, product = over_rows(first_sums, (zeros, zeros))

    norm_before = step_before = None
    for turn in range(ITERS):
        last = turn == ITERS - 1
        send_sums(turn, norm, product)
        if not last:
            send_edges(turn)
            close_ends(searched, zeros)
            edges_here(turn)
            operate(lambda block, k: edges[turn, 0, 2 * block + k], lambda block, k: edges[turn, 1, 2 * block + k])
        norm_now, product_now = sums_here(turn)
        if turn == 0:
            step_size = norm_now / product_now
        else:
            ratio = norm_now / norm_before
            step_size = norm_now / (product_now - ratio * norm_now / step_before)
        norm_before, step_before = norm_now, step_size

        def update(block, k, carry):
            row = 2 * block + k
            norm, product = carry
            residual_here, image_here = residual[:, row], searched[:, row + 1]
            direction_here, along_here, beyond_here = residual_here, image_here, image[:, row]
            answer_here = step_size * direction_here
            if turn > 0:
                direction_here = direction_here + ratio * direction[:, row]
                along_here = along_here + ratio * along[:, row]
                beyond_here = beyond_here + ratio * beyond[:, row]
                answer_here = answer[:, row] + step_size * direction_here
            residual_here = residual_here - step_size * along_here
            image_here = image_here - step_size * beyond_here
            answer[:, row] = answer_here
            direction[:, row] = direction_here
            along[:, row] = along_here
            beyond[:, row] = beyond_here
            residual[:, row] = residual_here
            searched[:, row + 1] = image_here
            return norm + jnp.sum(residual_here * residual_here, axis=0), product + jnp.sum(
                residual_here * image_here, axis=0
            )

        def finish(block, k, carry):
            row = 2 * block + k
            answer[:, row] = answer[:, row] + step_size * (residual[:, row] + ratio * direction[:, row])
            return carry

        if last:
            over_rows(finish, 0)
        else:
            edges_sent(turn)
            norm, product = over_rows(update, (zeros, zeros))

    for block in range(HALF // 2):
        chosen = two_rows(held_wanted[block], held_wanted[HALF // 2 + block])
        value = zeros
        for choice in range(8):
            value = value + jnp.where(chosen == choice, answer[choice % 4, 2 * block + choice // 4], 0.0)
        picked[block] = value[:4]
        picked[HALF // 2 + block] = value[4:]

    returned[space] = picked[space]
    for step in range(1, SPACE):
        other, device = space_peer(step)
        pltpu.make_async_remote_copy(
            src_ref=picked.at[other],
            dst_ref=returned.at[space],
            send_sem=swap_send.at[3],
            recv_sem=swap_recv.at[3],
            device_id=device,
            device_id_type=pl.DeviceIdType.MESH,
        ).start()
    wait_bytes(returned.at[pl.ds(0, others)], swap_recv.at[3])
    for i in range(SPACE // 2):
        predicted[pl.ds(8 * i, 8)] = jnp.concatenate([returned[2 * i], returned[2 * i + 1]])

    values = predicted[...]
    inverse_sigma = 1.0 / jnp.sqrt(obs_var[...])
    spread = (values - jnp.mean(values, axis=0, keepdims=True)) * inverse_sigma
    misfit = (obs_values[...] - values) * inverse_sigma + obs_noise[...]
    for i, other in enumerate((spread, misfit)):
        product = lax.dot_general(
            spread, other, (((1,), (1,)), ((), ())), precision=lax.Precision.HIGHEST, preferred_element_type=jnp.float32
        )
        for j in range(HALF):
            part[HALF * i + j] = product[4 * j : 4 * j + 4]
    sum_everywhere(part, total, *sum_refs)

    edges_sent(COND)
    edges_sent(SOURCE)
    for turn in range(ITERS):
        wait_bytes(tiles.at[turn, pl.ds(0, TEAM - 1)], tile_send.at[turn])
    wait_bytes(ensemble.at[pl.ds(0, others * 32)], swap_send.at[0])
    wait_bytes(ensemble.at[pl.ds(0, others * 8)], swap_send.at[1])
    wait_bytes(held_wanted.at[pl.ds(0, others)], swap_send.at[2])
    wait_bytes(returned.at[pl.ds(0, others)], swap_send.at[3])


def predict(ensemble, source, wanted, obs_values, obs_noise, obs_var):
    held = (4, HALF, 8, 128)
    padded = (4, HALF + 2, 8, 128)
    vmem = lambda *shape: pltpu.VMEM(shape, jnp.float32)
    return pl.pallas_call(
        conjugate_kernel,
        out_shape=[jax.ShapeDtypeStruct((rows, 128), jnp.float32) for rows in (128, 256)],
        in_specs=[pl.BlockSpec(memory_space=pl.ANY), *[pl.BlockSpec(memory_space=pltpu.VMEM)] * 5],
        out_specs=[pl.BlockSpec(memory_space=pltpu.VMEM)] * 2,
        scratch_shapes=[
            vmem(HALF // 2, 64, 128),
            vmem(HALF // 2, 16, 128),
            pltpu.VMEM((SPACE, 1, 128), jnp.int32),
            vmem(SPACE, 4, 128),
            vmem(SPACE, 4, 128),
            vmem(2, HALF // 2, 4, 128),
            vmem(*padded),
            vmem(4, HALF + 1, 8, 128),
            vmem(5, HALF, 8, 128),
            vmem(*held),
            vmem(*held),
            vmem(*padded),
            *[vmem(*held)] * 6,
            vmem(2, HALF, 8, 128),
            vmem(2, HALF // 2, 4, 128),
            vmem(ITERS - 1, 2, HALF, 8, 128),
            vmem(ITERS, TEAM, 8, 128),
            pltpu.SemaphoreType.DMA((ITERS + 1, 2)),
            pltpu.SemaphoreType.DMA((ITERS + 1, 2)),
            pltpu.SemaphoreType.DMA((ITERS,)),
            pltpu.SemaphoreType.DMA((ITERS,)),
            pltpu.SemaphoreType.DMA((4,)),
            pltpu.SemaphoreType.DMA((4,)),
            pltpu.SemaphoreType.DMA((3,)),
            vmem(64, 4, 128),
            vmem(WIDE - 1, WIDE, 4, 128),
            vmem(WIDE, 4, 128),
            vmem(WIDE - 1, 4, 128),
            vmem(4, 128),
            vmem(WIDE, 4, 128),
            vmem(WIDE, 4, 128),
            vmem(WIDE, WIDE, 4, 128),
            pltpu.SemaphoreType.DMA((5, WIDE - 1)),
            pltpu.SemaphoreType.DMA((5, WIDE - 1)),
        ],
        compiler_params=pltpu.CompilerParams(collective_id=2, has_side_effects=True),
        name="predict",
    )(ensemble, source, wanted, obs_values, obs_noise, obs_var)


PANEL = 8


def solve_kernel(total, ensemble, updated, gram, cross, scaled, weights):
    plane = (PANEL, 128)
    count = gram.shape[0]
    sublane = lax.broadcasted_iota(jnp.int32, plane, 0)
    lane = lax.broadcasted_iota(jnp.int32, plane, 1)
    whole = functools.partial(lax.dot_general, precision=lax.Precision.HIGHEST, preferred_element_type=jnp.float32)

    def spread(row):
        return jnp.broadcast_to(row, plane)

    for low in range(0, count, PANEL):
        gram[low : low + PANEL] = total[low : low + PANEL] + jnp.where(lane == sublane + low, count - 1.0, 0.0)
    cross[...] = total[count:]

    for low in range(0, count, PANEL):
        rows_g, rows_c = gram[low : low + PANEL], cross[low : low + PANEL]
        columns = [spread(rows_g[:, low + j : low + j + 1]) for j in range(PANEL)]
        pivots = {(i, j): spread(columns[j][i : i + 1]) for j in range(PANEL) for i in range(j + 1)}
        inverse, factor = [], {}
        for k in range(PANEL):
            inverse.append(1.0 / pivots[k, k])
            for i in range(k + 1, PANEL):
                factor[i, k] = pivots[k, i] * inverse[k]
                for j in range(i, PANEL):
                    pivots[i, j] = pivots[i, j] - factor[i, k] * pivots[k, j]
        solved = []
        for rows in (rows_g, rows_c):
            lines = [spread(rows[i : i + 1]) for i in range(PANEL)]
            for k in range(PANEL):
                for i in range(k + 1, PANEL):
                    lines[i] = lines[i] - factor[i, k] * lines[k]
            lines = [line * inverse[i] for i, line in enumerate(lines)]
            for k in reversed(range(PANEL)):
                for i in range(k):
                    lines[i] = lines[i] - factor[k, i] * lines[k]
            joined = lines[0]
            for i in range(1, PANEL):
                joined = jnp.where(sublane == i, lines[i], joined)
            solved.append(joined)
        scaled[low : low + PANEL] = solved[0]
        weights[low : low + PANEL] = solved[1]
        after = low + PANEL
        if after < count:
            taken = rows_g.T
            gram[after:] = gram[after:] - whole(taken, solved[0], (((1,), (0,)), ((), ())))[after:]
            cross[after:] = cross[after:] - whole(taken, solved[1], (((1,), (0,)), ((), ())))[after:]

    for low in range(count - 2 * PANEL, -1, -PANEL):
        known = low + PANEL
        left = jnp.where(lane >= known, scaled[low : low + PANEL], 0.0)
        weights[low : low + PANEL] = weights[low : low + PANEL] - whole(left, weights[...], (((1,), (0,)), ((), ())))

    turned = weights[...].T
    for row in range(PANEL):
        picks = [pl.ds(row + 8 * PANEL * i, PANEL, stride=8) for i in range(count // PANEL)]
        fields = [ensemble[pick, :] for pick in picks]
        mean = jnp.sum(sum(fields), axis=0, keepdims=True) * (1.0 / count)
        change = whole(turned, jnp.concatenate([field - mean for field in fields]), (((1,), (0,)), ((), ())))
        for i, pick in enumerate(picks):
            updated[pick, :] = fields[i] + change[PANEL * i : PANEL * (i + 1)]


def solve_and_update(total, ensemble):
    square = pltpu.VMEM((total.shape[1], total.shape[1]), jnp.float32)
    return pl.pallas_call(
        solve_kernel,
        out_shape=jax.ShapeDtypeStruct(ensemble.shape, jnp.float32),
        in_specs=[pl.BlockSpec(memory_space=pltpu.VMEM)] * 2,
        out_specs=pl.BlockSpec(memory_space=pltpu.VMEM),
        scratch_shapes=[square] * 4,
        name="solve_and_update",
    )(total, ensemble)


def local(ensemble, source, obs_rows, obs_values, obs_noise, obs_var):
    layers = source.shape[-1]
    fields = ensemble.reshape(-1, layers)
    wanted = jnp.broadcast_to(obs_rows.reshape(1, 1), (1, layers))
    predicted, total = predict(
        fields,
        source.reshape(-1, layers),
        wanted,
        obs_values.reshape(1, layers),
        obs_noise.reshape(-1, layers),
        obs_var.reshape(1, layers),
    )
    updated = solve_and_update(total, fields)
    return (updated.reshape(ensemble.shape), predicted.reshape(obs_noise.shape))


def solution(mesh):
    in_specs = (
        P(None, "space", "member", None),
        P("space", "member", None),
        P("space", "member", None),
        P("space", "member", None),
        P(None, "space", "member", None),
        P("space", "member", None),
    )
    out_specs = (P(None, "space", "member", None), P(None, "space", "member", None))
    return jax.shard_map(local, mesh=mesh, in_specs=in_specs, out_specs=out_specs, check_vma=False)
```

```python
import functools

import jax
import jax.numpy as jnp
from jax import lax
from jax.experimental import pallas as pl
from jax.experimental.pallas import tpu as pltpu
from jax.sharding import PartitionSpec as P

X, Y_LO, Y_HI, Z, CORES = 4, 4, 2, 8, 2
WIDE = 8

ITERS = 4


def place():
    member = lax.axis_index("member")
    space = lax.axis_index("space")
    x = lax.rem(member, X)
    y = lax.div(space, Z * CORES) * Y_LO + lax.div(member, X)
    z = lax.rem(lax.div(space, CORES), Z)
    return x, y, z, lax.rem(space, CORES)


def device_at(x, y, z, core):
    member = lax.rem(y, Y_LO) * X + x
    space = (lax.div(y, Y_LO) * Z + z) * CORES + core
    return {"member": member, "space": space}


def sum_peers():
    x, y, z, core = place()
    row = x * CORES + core

    def row_peer(step):
        other = lax.rem(row + step, WIDE)
        return other, device_at(lax.div(other, CORES), y, z, lax.rem(other, CORES))

    def y_peer(step):
        other = lax.rem(y + step, WIDE)
        return other, device_at(x, other, z, core)

    def z_peer(step):
        other = lax.rem(z + step, WIDE)
        return other, device_at(x, y, other, core)

    return (row, y, z), (row_peer, y_peer, z_peer)


def sum_everywhere(part, total, got_row, sum_row, got_y, sum_y, got_z, all_y, all_row, send_sems, recv_sems):
    (row, y, z), (row_peer, y_peer, z_peer) = sum_peers()

    def exchange(phase, peer, source, target):
        copies = []
        for step in range(1, WIDE):
            other, device = peer(step)
            copy = pltpu.make_async_remote_copy(
                src_ref=source(other),
                dst_ref=target(step),
                send_sem=send_sems.at[phase, step - 1],
                recv_sem=recv_sems.at[phase, step - 1],
                device_id=device,
                device_id_type=pl.DeviceIdType.MESH,
            )
            copy.start()
            copies.append(copy)
        return copies

    def arrived(copies):
        for copy in copies:
            copy.wait_recv()

    sent = []
    copies = exchange(0, row_peer, lambda o: part.at[pl.ds(o * WIDE, WIDE)], lambda s: got_row.at[s - 1])
    sent += copies
    arrived(copies)
    sum_row[...] = part[pl.ds(row * WIDE, WIDE)] + jnp.sum(got_row[...], axis=0)

    copies = exchange(1, y_peer, lambda o: sum_row.at[o], lambda s: got_y.at[s - 1])
    sent += copies
    arrived(copies)
    sum_y[...] = sum_row[y] + jnp.sum(got_y[...], axis=0)

    got_z[z] = sum_y[...]
    copies = exchange(2, z_peer, lambda o: sum_y, lambda s: got_z.at[z])
    sent += copies
    arrived(copies)
    sum_y_z = jnp.sum(got_z[...], axis=0)
    all_y[y] = sum_y_z

    copies = exchange(3, y_peer, lambda o: all_y.at[y], lambda s: all_y.at[y])
    sent += copies
    arrived(copies)

    copies = exchange(4, row_peer, lambda o: all_y, lambda s: all_row.at[row])
    sent += copies
    all_row[row] = all_y[...]
    arrived(copies)
    for i in range(WIDE):
        for j in range(0, WIDE, 2):
            total[pl.ds(4 * (WIDE * i + j), 8)] = jnp.concatenate([all_row[i, j], all_row[i, j + 1]])
    for copy in sent:
        copy.wait_send()


def harmonic(first_cond, second_cond):
    return 2.0 * first_cond * second_cond / (first_cond + second_cond)


HALF = 32
TEAM = 16
SPACE = 32
COND, SOURCE = ITERS - 1, ITERS


def conjugate_kernel(
    ensemble,
    source,
    wanted,
    obs_values,
    obs_noise,
    obs_var,
    predicted,
    total,
    held_rows,
    held_source,
    held_wanted,
    picked,
    returned,
    side,
    cond,
    face_x,
    face_y,
    face_z,
    lower_z,
    searched,
    image,
    residual,
    direction,
    along,
    beyond,
    answer,
    cond_edge,
    source_edge,
    edges,
    tiles,
    edge_send,
    edge_recv,
    tile_send,
    tile_recv,
    swap_send,
    swap_recv,
    own_sems,
    part,
    *sum_refs,
):
    member = lax.axis_index("member")
    space = lax.axis_index("space")
    plane = (8, 128)
    sublane = lax.broadcasted_iota(jnp.int32, plane, 0)
    lane = lax.broadcasted_iota(jnp.int32, plane, 1)
    lane_4 = lax.broadcasted_iota(jnp.int32, (4, 8, 128), 2)
    low_half = sublane < 4

    def team_peer(step):
        return {"member": lax.rem(member + step, TEAM)}

    def edge_copy(kind, upward):
        if kind == COND:
            origin, target = cond.at[3 * upward, pl.ds(1, HALF)], cond_edge.at[1 - upward]
        elif kind == SOURCE:
            origin, target = side.at[upward], source_edge.at[1 - upward]
        else:
            origin, target = searched.at[3 * upward, pl.ds(1, HALF)], edges.at[kind, 1 - upward]
        return pltpu.make_async_remote_copy(
            src_ref=origin,
            dst_ref=target,
            send_sem=edge_send.at[kind, upward],
            recv_sem=edge_recv.at[kind, 1 - upward],
            device_id=team_peer(1 if upward else TEAM - 1),
            device_id_type=pl.DeviceIdType.MESH,
        )

    def send_edges(kind):
        @pl.when(member > 0)
        def _():
            edge_copy(kind, 0).start()

        @pl.when(member < TEAM - 1)
        def _():
            edge_copy(kind, 1).start()

    def edges_sent(kind):
        @pl.when(member > 0)
        def _():
            edge_copy(kind, 0).wait_send()

        @pl.when(member < TEAM - 1)
        def _():
            edge_copy(kind, 1).wait_send()

    def edges_here(kind):
        @pl.when(member > 0)
        def _():
            edge_copy(kind, 1).wait_recv()

        @pl.when(member < TEAM - 1)
        def _():
            edge_copy(kind, 0).wait_recv()

    def tile_copy(turn, step):
        return pltpu.make_async_remote_copy(
            src_ref=tiles.at[turn, member],
            dst_ref=tiles.at[turn, member],
            send_sem=tile_send.at[turn],
            recv_sem=tile_recv.at[turn],
            device_id=team_peer(step),
            device_id_type=pl.DeviceIdType.MESH,
        )

    def wait_bytes(ref, sem):
        pltpu.make_async_copy(ref, ref, sem).wait()

    def space_peer(step):
        other = lax.rem(space + step, SPACE)
        return other, {"space": other}

    def halves(index):
        return lax.rem(index, HALF // 2), lax.div(index, HALF // 2)

    def piece_refs(other):
        block, half = halves(space)
        rows = pl.ds(pl.multiple_of(half * 32, 32), 32)
        return (
            (ensemble.at[pl.ds(pl.multiple_of(other * 32, 32), 32)], held_rows.at[block, rows]),
            (source, held_source.at[block, pl.ds(pl.multiple_of(half * 8, 8), 8)]),
            (wanted, held_wanted.at[space]),
        )

    def swap(step):
        other, device = space_peer(step)
        for kind, (origin, target) in enumerate(piece_refs(other)):
            pltpu.make_async_remote_copy(
                src_ref=origin,
                dst_ref=target,
                send_sem=swap_send.at[kind],
                recv_sem=swap_recv.at[kind],
                device_id=device,
                device_id_type=pl.DeviceIdType.MESH,
            ).start()

    def send_sums(turn, norm, product):
        norm = norm + pltpu.roll(norm, 64, 1)
        product = product + pltpu.roll(product, 64, 1)
        both = jnp.where(lane < 64, norm, product)
        tiles[turn, member] = both[:4] + both[4:]
        for step in range(1, TEAM):
            tile_copy(turn, step).start()

    def sums_here(turn):
        wait_bytes(tiles.at[turn, pl.ds(0, TEAM - 1)], tile_recv.at[turn])
        both = jnp.sum(tiles[turn], axis=0)
        both = jnp.concatenate([both, both])
        norm = jnp.sum(jnp.where(lane < 64, both, 0.0), axis=1, keepdims=True)
        product = jnp.sum(jnp.where(lane < 64, 0.0, both), axis=1, keepdims=True)
        return jnp.broadcast_to(norm, plane), jnp.broadcast_to(product, plane)

    def over_rows(body, start):
        def several(block, carry):
            for k in range(2):
                carry = body(block, k, carry)
            return carry

        return lax.fori_loop(0, HALF // 2, several, start)

    barrier = pltpu.get_barrier_semaphore()
    for step in range(1, SPACE):
        pl.semaphore_signal(barrier, inc=1, device_id=space_peer(step)[1], device_id_type=pl.DeviceIdType.MESH)
    for step in range(1, TEAM):
        pl.semaphore_signal(barrier, inc=1, device_id=team_peer(step), device_id_type=pl.DeviceIdType.MESH)
    for peer in sum_peers()[1]:
        for step in range(1, WIDE):
            pl.semaphore_signal(barrier, inc=1, device_id=peer(step)[1], device_id_type=pl.DeviceIdType.MESH)
    own = [
        pltpu.make_async_copy(origin, target, own_sems.at[kind])
        for kind, (origin, target) in enumerate(piece_refs(space))
    ]
    for copy in own:
        copy.start()
    pl.semaphore_wait(barrier, TEAM - 1 + SPACE - 1 + 3 * (WIDE - 1))
    for step in range(1, SPACE):
        swap(step)

    @pl.when(member == 0)
    def _():
        source_edge[0] = jnp.zeros(source_edge.shape[1:], jnp.float32)
        for kind in range(ITERS - 1):
            edges[kind, 0] = jnp.zeros(edges.shape[2:], jnp.float32)

    @pl.when(member == TEAM - 1)
    def _():
        source_edge[1] = jnp.zeros(source_edge.shape[1:], jnp.float32)
        for kind in range(ITERS - 1):
            edges[kind, 1] = jnp.zeros(edges.shape[2:], jnp.float32)

    for copy in own:
        copy.wait()
    others = SPACE - 1
    wait_bytes(ensemble.at[pl.ds(0, others * 32)], swap_recv.at[0])
    wait_bytes(ensemble.at[pl.ds(0, others * 8)], swap_recv.at[1])
    wait_bytes(held_wanted.at[pl.ds(0, others)], swap_recv.at[2])

    def two_rows(lower, upper):
        return jnp.where(low_half, jnp.broadcast_to(lower, plane), jnp.broadcast_to(upper, plane))

    def close_ends(padded, outside):
        for y in range(4):
            first, last = padded[y, 1], padded[y, HALF]
            below = first if outside is None else outside
            above = last if outside is None else outside
            padded[y, 0] = jnp.where(low_half, below, pltpu.roll(last, 4, 0))
            padded[y, HALF + 1] = jnp.where(low_half, pltpu.roll(first, 4, 0), above)

    def begin(block, carry):
        rows = held_source[block]
        for k in range(2):
            for y in range(4):
                at = 4 * k + y
                held = held_rows[block, pl.ds(at, 8, stride=8), :]
                cond[y, 2 * block + k + 1] = jnp.exp(held)
                searched[y, 2 * block + k + 1] = two_rows(rows[at : at + 1], rows[8 + at : 9 + at])
        for upward in range(2):
            at = 3 * upward
            side[upward, block] = jnp.concatenate([rows[at + k : at + k + 1] for k in (0, 8, 4, 12)])
        return carry

    lax.fori_loop(0, HALF // 2, begin, 0)
    send_edges(COND)
    send_edges(SOURCE)
    close_ends(cond, None)
    close_ends(searched, jnp.zeros(plane, jnp.float32))

    @pl.when(member == 0)
    def _():
        cond_edge[0] = cond[0, pl.ds(1, HALF)]

    @pl.when(member == TEAM - 1)
    def _():
        cond_edge[1] = cond[3, pl.ds(1, HALF)]

    def inner_faces(block, k, carry):
        row = 2 * block + k
        here = cond[:, row + 1]
        face_x[:, row + 1] = harmonic(here, cond[:, row + 2])
        above = jnp.where(lane_4 == 127, here, pltpu.roll(here, 127, 2))
        upper = harmonic(here, above)
        face_z[:, row] = upper
        lower_z[:, row] = jnp.where(lane_4 == 0, here, pltpu.roll(upper, 1, 2))
        face_y[1:4, row] = harmonic(here[:3], here[1:])
        face_y[0, row] = here[0]
        face_y[4, row] = here[3]
        return carry

    over_rows(inner_faces, 0)
    for y in range(4):
        face_x[y, 0] = harmonic(cond[y, 0], cond[y, 1])

    def outer_faces(block, k, carry):
        row = 2 * block + k
        face_y[0, row] = harmonic(cond_edge[0, row], cond[0, row + 1])
        face_y[4, row] = harmonic(cond[3, row + 1], cond_edge[1, row])
        return carry

    def operate():
        def body(block, k, carry):
            row = 2 * block + k
            here = searched[:, row + 1]
            before = jnp.concatenate([here[:1], here[:3]])
            after = jnp.concatenate([here[1:], here[3:]])
            result = face_x[:, row + 1] * (here - searched[:, row + 2])
            result = result + face_x[:, row] * (here - searched[:, row])
            result = result + face_y[1:5, row] * (here - after)
            result = result + face_y[0:4, row] * (here - before)
            above = jnp.where(lane_4 == 127, 0.0, pltpu.roll(here, 127, 2))
            below = jnp.where(lane_4 == 0, 0.0, pltpu.roll(here, 1, 2))
            result = result + face_z[:, row] * (here - above)
            image[:, row] = result + lower_z[:, row] * (here - below)
            return carry

        over_rows(body, 0)

    def operate_edges(lower_edge, upper_edge):
        def body(block, k, carry):
            row = 2 * block + k
            image[0, row] = image[0, row] + face_y[0, row] * (searched[0, row + 1] - lower_edge(block, k))
            image[3, row] = image[3, row] + face_y[4, row] * (searched[3, row + 1] - upper_edge(block, k))
            return carry

        over_rows(body, 0)

    def over_planes(body, kind):
        def outer(block, k, carry):
            return body(slice(3, 4), 2 * block + k, body(slice(0, 1), 2 * block + k, carry))

        def inner(block, k, carry):
            return body(slice(1, 3), 2 * block + k, carry)

        sums = over_rows(outer, (zeros, zeros))
        if kind < ITERS - 1:
            send_edges(kind)
        return over_rows(inner, sums)

    zeros = jnp.zeros(plane, jnp.float32)
    operate()
    edges_here(COND)
    over_rows(outer_faces, 0)
    edges_here(SOURCE)

    def source_side(upward):
        def rows(block, k):
            four = source_edge[upward, block]
            return two_rows(four[2 * k : 2 * k + 1], four[2 * k + 1 : 2 * k + 2])

        return rows

    operate_edges(source_side(0), source_side(1))

    def first_sums(ys, row, carry):
        norm, product = carry
        image_here = image[ys, row]
        residual_here = searched[ys, row + 1]
        residual[ys, row] = residual_here
        searched[ys, row + 1] = image_here
        return norm + jnp.sum(residual_here * residual_here, axis=0), product + jnp.sum(
            residual_here * image_here, axis=0
        )

    norm, product = over_planes(first_sums, 0)

    norm_before = step_before = None
    for turn in range(ITERS):
        last = turn == ITERS - 1
        send_sums(turn, norm, product)
        if not last:
            close_ends(searched, zeros)
            operate()
            edges_here(turn)
            operate_edges(
                lambda block, k: edges[turn, 0, 2 * block + k], lambda block, k: edges[turn, 1, 2 * block + k]
            )
        norm_now, product_now = sums_here(turn)
        if turn == 0:
            step_size = norm_now / product_now
        else:
            ratio = norm_now / norm_before
            step_size = norm_now / (product_now - ratio * norm_now / step_before)
        norm_before, step_before = norm_now, step_size

        def update(ys, row, carry):
            norm, product = carry
            residual_here, image_here = residual[ys, row], searched[ys, row + 1]
            direction_here, along_here, beyond_here = residual_here, image_here, image[ys, row]
            answer_here = step_size * direction_here
            if turn > 0:
                direction_here = direction_here + ratio * direction[ys, row]
                along_here = along_here + ratio * along[ys, row]
                beyond_here = beyond_here + ratio * beyond[ys, row]
                answer_here = answer[ys, row] + step_size * direction_here
            residual_here = residual_here - step_size * along_here
            image_here = image_here - step_size * beyond_here
            answer[ys, row] = answer_here
            direction[ys, row] = direction_here
            along[ys, row] = along_here
            beyond[ys, row] = beyond_here
            residual[ys, row] = residual_here
            searched[ys, row + 1] = image_here
            return norm + jnp.sum(residual_here * residual_here, axis=0), product + jnp.sum(
                residual_here * image_here, axis=0
            )

        def finish(block, k, carry):
            row = 2 * block + k
            answer[:, row] = answer[:, row] + step_size * (residual[:, row] + ratio * direction[:, row])
            return carry

        if last:
            over_rows(finish, 0)
        else:
            edges_sent(turn)
            norm, product = over_planes(update, turn + 1)

    for block in range(HALF // 2):
        chosen = two_rows(held_wanted[block], held_wanted[HALF // 2 + block])
        value = zeros
        for choice in range(8):
            value = value + jnp.where(chosen == choice, answer[choice % 4, 2 * block + choice // 4], 0.0)
        picked[block] = value[:4]
        picked[HALF // 2 + block] = value[4:]

    returned[space] = picked[space]
    for step in range(1, SPACE):
        other, device = space_peer(step)
        pltpu.make_async_remote_copy(
            src_ref=picked.at[other],
            dst_ref=returned.at[space],
            send_sem=swap_send.at[3],
            recv_sem=swap_recv.at[3],
            device_id=device,
            device_id_type=pl.DeviceIdType.MESH,
        ).start()
    wait_bytes(returned.at[pl.ds(0, others)], swap_recv.at[3])
    for i in range(SPACE // 2):
        predicted[pl.ds(8 * i, 8)] = jnp.concatenate([returned[2 * i], returned[2 * i + 1]])

    values = predicted[...]
    inverse_sigma = 1.0 / jnp.sqrt(obs_var[...])
    spread = (values - jnp.mean(values, axis=0, keepdims=True)) * inverse_sigma
    misfit = (obs_values[...] - values) * inverse_sigma + obs_noise[...]
    for i, other in enumerate((spread, misfit)):
        product = lax.dot_general(
            spread, other, (((1,), (1,)), ((), ())), precision=lax.Precision.HIGHEST, preferred_element_type=jnp.float32
        )
        for j in range(HALF):
            part[HALF * i + j] = product[4 * j : 4 * j + 4]
    sum_everywhere(part, total, *sum_refs)

    edges_sent(COND)
    edges_sent(SOURCE)
    for turn in range(ITERS):
        wait_bytes(tiles.at[turn, pl.ds(0, TEAM - 1)], tile_send.at[turn])
    wait_bytes(ensemble.at[pl.ds(0, others * 32)], swap_send.at[0])
    wait_bytes(ensemble.at[pl.ds(0, others * 8)], swap_send.at[1])
    wait_bytes(held_wanted.at[pl.ds(0, others)], swap_send.at[2])
    wait_bytes(returned.at[pl.ds(0, others)], swap_send.at[3])


def predict(ensemble, source, wanted, obs_values, obs_noise, obs_var):
    held = (4, HALF, 8, 128)
    padded = (4, HALF + 2, 8, 128)
    vmem = lambda *shape: pltpu.VMEM(shape, jnp.float32)
    return pl.pallas_call(
        conjugate_kernel,
        out_shape=[jax.ShapeDtypeStruct((rows, 128), jnp.float32) for rows in (128, 256)],
        in_specs=[pl.BlockSpec(memory_space=pl.ANY), *[pl.BlockSpec(memory_space=pltpu.VMEM)] * 5],
        out_specs=[pl.BlockSpec(memory_space=pltpu.VMEM)] * 2,
        scratch_shapes=[
            vmem(HALF // 2, 64, 128),
            vmem(HALF // 2, 16, 128),
            pltpu.VMEM((SPACE, 1, 128), jnp.int32),
            vmem(SPACE, 4, 128),
            vmem(SPACE, 4, 128),
            vmem(2, HALF // 2, 4, 128),
            vmem(*padded),
            vmem(4, HALF + 1, 8, 128),
            vmem(5, HALF, 8, 128),
            vmem(*held),
            vmem(*held),
            vmem(*padded),
            *[vmem(*held)] * 6,
            vmem(2, HALF, 8, 128),
            vmem(2, HALF // 2, 4, 128),
            vmem(ITERS - 1, 2, HALF, 8, 128),
            vmem(ITERS, TEAM, 4, 128),
            pltpu.SemaphoreType.DMA((ITERS + 1, 2)),
            pltpu.SemaphoreType.DMA((ITERS + 1, 2)),
            pltpu.SemaphoreType.DMA((ITERS,)),
            pltpu.SemaphoreType.DMA((ITERS,)),
            pltpu.SemaphoreType.DMA((4,)),
            pltpu.SemaphoreType.DMA((4,)),
            pltpu.SemaphoreType.DMA((3,)),
            vmem(64, 4, 128),
            vmem(WIDE - 1, WIDE, 4, 128),
            vmem(WIDE, 4, 128),
            vmem(WIDE - 1, 4, 128),
            vmem(4, 128),
            vmem(WIDE, 4, 128),
            vmem(WIDE, 4, 128),
            vmem(WIDE, WIDE, 4, 128),
            pltpu.SemaphoreType.DMA((5, WIDE - 1)),
            pltpu.SemaphoreType.DMA((5, WIDE - 1)),
        ],
        compiler_params=pltpu.CompilerParams(collective_id=2, has_side_effects=True),
        name="predict",
    )(ensemble, source, wanted, obs_values, obs_noise, obs_var)


PANEL = 8


def solve_kernel(total, ensemble, updated, gram, cross, scaled, weights):
    plane = (PANEL, 128)
    count = gram.shape[0]
    sublane = lax.broadcasted_iota(jnp.int32, plane, 0)
    lane = lax.broadcasted_iota(jnp.int32, plane, 1)
    whole = functools.partial(lax.dot_general, precision=lax.Precision.HIGHEST, preferred_element_type=jnp.float32)

    def spread(row):
        return jnp.broadcast_to(row, plane)

    for low in range(0, count, PANEL):
        gram[low : low + PANEL] = total[low : low + PANEL] + jnp.where(lane == sublane + low, count - 1.0, 0.0)
    cross[...] = total[count:]

    for low in range(0, count, PANEL):
        rows_g, rows_c = gram[low : low + PANEL], cross[low : low + PANEL]
        columns = [spread(rows_g[:, low + j : low + j + 1]) for j in range(PANEL)]
        pivots = {(i, j): spread(columns[j][i : i + 1]) for j in range(PANEL) for i in range(j + 1)}
        inverse, factor = [], {}
        for k in range(PANEL):
            inverse.append(1.0 / pivots[k, k])
            for i in range(k + 1, PANEL):
                factor[i, k] = pivots[k, i] * inverse[k]
                for j in range(i, PANEL):
                    pivots[i, j] = pivots[i, j] - factor[i, k] * pivots[k, j]
        solved = []
        for rows in (rows_g, rows_c):
            lines = [spread(rows[i : i + 1]) for i in range(PANEL)]
            for k in range(PANEL):
                for i in range(k + 1, PANEL):
                    lines[i] = lines[i] - factor[i, k] * lines[k]
            lines = [line * inverse[i] for i, line in enumerate(lines)]
            for k in reversed(range(PANEL)):
                for i in range(k):
                    lines[i] = lines[i] - factor[k, i] * lines[k]
            joined = lines[0]
            for i in range(1, PANEL):
                joined = jnp.where(sublane == i, lines[i], joined)
            solved.append(joined)
        scaled[low : low + PANEL] = solved[0]
        weights[low : low + PANEL] = solved[1]
        after = low + PANEL
        if after < count:
            taken = rows_g.T
            gram[after:] = gram[after:] - whole(taken, solved[0], (((1,), (0,)), ((), ())))[after:]
            cross[after:] = cross[after:] - whole(taken, solved[1], (((1,), (0,)), ((), ())))[after:]

    for low in range(count - 2 * PANEL, -1, -PANEL):
        known = low + PANEL
        left = jnp.where(lane >= known, scaled[low : low + PANEL], 0.0)
        weights[low : low + PANEL] = weights[low : low + PANEL] - whole(left, weights[...], (((1,), (0,)), ((), ())))

    turned = weights[...].T
    for row in range(PANEL):
        picks = [pl.ds(row + 8 * PANEL * i, PANEL, stride=8) for i in range(count // PANEL)]
        fields = [ensemble[pick, :] for pick in picks]
        mean = jnp.sum(sum(fields), axis=0, keepdims=True) * (1.0 / count)
        change = whole(turned, jnp.concatenate([field - mean for field in fields]), (((1,), (0,)), ((), ())))
        for i, pick in enumerate(picks):
            updated[pick, :] = fields[i] + change[PANEL * i : PANEL * (i + 1)]


def solve_and_update(total, ensemble):
    square = pltpu.VMEM((total.shape[1], total.shape[1]), jnp.float32)
    return pl.pallas_call(
        solve_kernel,
        out_shape=jax.ShapeDtypeStruct(ensemble.shape, jnp.float32),
        in_specs=[pl.BlockSpec(memory_space=pltpu.VMEM)] * 2,
        out_specs=pl.BlockSpec(memory_space=pltpu.VMEM),
        scratch_shapes=[square] * 4,
        name="solve_and_update",
    )(total, ensemble)


def local(ensemble, source, obs_rows, obs_values, obs_noise, obs_var):
    layers = source.shape[-1]
    fields = ensemble.reshape(-1, layers)
    wanted = jnp.broadcast_to(obs_rows.reshape(1, 1), (1, layers))
    predicted, total = predict(
        fields,
        source.reshape(-1, layers),
        wanted,
        obs_values.reshape(1, layers),
        obs_noise.reshape(-1, layers),
        obs_var.reshape(1, layers),
    )
    updated = solve_and_update(total, fields)
    return (updated.reshape(ensemble.shape), predicted.reshape(obs_noise.shape))


def solution(mesh):
    in_specs = (
        P(None, "space", "member", None),
        P("space", "member", None),
        P("space", "member", None),
        P("space", "member", None),
        P(None, "space", "member", None),
        P("space", "member", None),
    )
    out_specs = (P(None, "space", "member", None), P(None, "space", "member", None))
    return jax.shard_map(local, mesh=mesh, in_specs=in_specs, out_specs=out_specs, check_vma=False)
```

```python
import functools

import jax
import jax.numpy as jnp
from jax import lax
from jax.experimental import pallas as pl
from jax.experimental.pallas import tpu as pltpu
from jax.sharding import PartitionSpec as P

X, Y_LO, Y_HI, Z, CORES = 4, 4, 2, 8, 2
WIDE = 8

ITERS = 4


def place():
    member = lax.axis_index("member")
    space = lax.axis_index("space")
    x = lax.rem(member, X)
    y = lax.div(space, Z * CORES) * Y_LO + lax.div(member, X)
    z = lax.rem(lax.div(space, CORES), Z)
    return x, y, z, lax.rem(space, CORES)


def device_at(x, y, z, core):
    member = lax.rem(y, Y_LO) * X + x
    space = (lax.div(y, Y_LO) * Z + z) * CORES + core
    return {"member": member, "space": space}


def sum_peers():
    x, y, z, core = place()
    row = x * CORES + core

    def row_peer(step):
        other = lax.rem(row + step, WIDE)
        return other, device_at(lax.div(other, CORES), y, z, lax.rem(other, CORES))

    def y_peer(step):
        other = lax.rem(y + step, WIDE)
        return other, device_at(x, other, z, core)

    def z_peer(step):
        other = lax.rem(z + step, WIDE)
        return other, device_at(x, y, other, core)

    return (row, y, z), (row_peer, y_peer, z_peer)


def sum_everywhere(part, total, got_row, sum_row, got_y, sum_y, got_z, all_y, all_row, send_sems, recv_sems):
    (row, y, z), (row_peer, y_peer, z_peer) = sum_peers()

    def exchange(phase, peer, source, target):
        copies = []
        for step in range(1, WIDE):
            other, device = peer(step)
            copy = pltpu.make_async_remote_copy(
                src_ref=source(other),
                dst_ref=target(step),
                send_sem=send_sems.at[phase, step - 1],
                recv_sem=recv_sems.at[phase, step - 1],
                device_id=device,
                device_id_type=pl.DeviceIdType.MESH,
            )
            copy.start()
            copies.append(copy)
        return copies

    def arrived(copies):
        for copy in copies:
            copy.wait_recv()

    sent = []
    copies = exchange(0, row_peer, lambda o: part.at[pl.ds(o * WIDE, WIDE)], lambda s: got_row.at[s - 1])
    sent += copies
    arrived(copies)
    sum_row[...] = part[pl.ds(row * WIDE, WIDE)] + jnp.sum(got_row[...], axis=0)

    copies = exchange(1, y_peer, lambda o: sum_row.at[o], lambda s: got_y.at[s - 1])
    sent += copies
    arrived(copies)
    sum_y[...] = sum_row[y] + jnp.sum(got_y[...], axis=0)

    got_z[z] = sum_y[...]
    copies = exchange(2, z_peer, lambda o: sum_y, lambda s: got_z.at[z])
    sent += copies
    arrived(copies)
    sum_y_z = jnp.sum(got_z[...], axis=0)
    all_y[y] = sum_y_z

    copies = exchange(3, y_peer, lambda o: all_y.at[y], lambda s: all_y.at[y])
    sent += copies
    arrived(copies)

    copies = exchange(4, row_peer, lambda o: all_y, lambda s: all_row.at[row])
    sent += copies
    all_row[row] = all_y[...]
    arrived(copies)
    for i in range(WIDE):
        for j in range(0, WIDE, 2):
            total[pl.ds(4 * (WIDE * i + j), 8)] = jnp.concatenate([all_row[i, j], all_row[i, j + 1]])
    for copy in sent:
        copy.wait_send()


def harmonic(first_cond, second_cond):
    return 2.0 * first_cond * second_cond / (first_cond + second_cond)


HALF = 32
TEAM = 16
SPACE = 32
COND, SOURCE = ITERS - 1, ITERS


def conjugate_kernel(
    ensemble,
    source,
    wanted,
    obs_values,
    obs_noise,
    obs_var,
    predicted,
    total,
    held_rows,
    held_source,
    held_wanted,
    picked,
    returned,
    side,
    cond,
    face_x,
    face_y,
    face_z,
    lower_z,
    searched,
    image,
    residual,
    direction,
    along,
    beyond,
    answer,
    cond_edge,
    source_edge,
    edges,
    tiles,
    edge_send,
    edge_recv,
    tile_send,
    tile_recv,
    swap_send,
    swap_recv,
    own_sems,
    relay_send,
    relay_recv,
    part,
    *sum_refs,
):
    member = lax.axis_index("member")
    space = lax.axis_index("space")
    plane = (8, 128)
    sublane = lax.broadcasted_iota(jnp.int32, plane, 0)
    lane = lax.broadcasted_iota(jnp.int32, plane, 1)
    lane_4 = lax.broadcasted_iota(jnp.int32, (4, 8, 128), 2)
    low_half = sublane < 4

    def team_peer(step):
        return {"member": lax.rem(member + step, TEAM)}

    def edge_copy(kind, upward):
        if kind == COND:
            origin, target = cond.at[3 * upward, pl.ds(1, HALF)], cond_edge.at[1 - upward]
        elif kind == SOURCE:
            origin, target = side.at[upward], source_edge.at[1 - upward]
        else:
            origin, target = searched.at[3 * upward, pl.ds(1, HALF)], edges.at[kind, 1 - upward]
        return pltpu.make_async_remote_copy(
            src_ref=origin,
            dst_ref=target,
            send_sem=edge_send.at[kind, upward],
            recv_sem=edge_recv.at[kind, 1 - upward],
            device_id=team_peer(1 if upward else TEAM - 1),
            device_id_type=pl.DeviceIdType.MESH,
        )

    def send_edges(kind):
        @pl.when(member > 0)
        def _():
            edge_copy(kind, 0).start()

        @pl.when(member < TEAM - 1)
        def _():
            edge_copy(kind, 1).start()

    def edges_sent(kind):
        @pl.when(member > 0)
        def _():
            edge_copy(kind, 0).wait_send()

        @pl.when(member < TEAM - 1)
        def _():
            edge_copy(kind, 1).wait_send()

    def edges_here(kind):
        @pl.when(member > 0)
        def _():
            edge_copy(kind, 1).wait_recv()

        @pl.when(member < TEAM - 1)
        def _():
            edge_copy(kind, 0).wait_recv()

    def tile_copy(turn, step):
        return pltpu.make_async_remote_copy(
            src_ref=tiles.at[turn, member],
            dst_ref=tiles.at[turn, member],
            send_sem=tile_send.at[turn],
            recv_sem=tile_recv.at[turn],
            device_id=team_peer(step),
            device_id_type=pl.DeviceIdType.MESH,
        )

    def wait_bytes(ref, sem):
        pltpu.make_async_copy(ref, ref, sem).wait()

    def space_peer(step):
        other = lax.rem(space + step, SPACE)
        return other, {"space": other}

    def halves(index):
        return lax.rem(index, HALF // 2), lax.div(index, HALF // 2)

    def piece_refs(other):
        block, half = halves(space)
        rows = pl.ds(pl.multiple_of(half * 32, 32), 32)
        return (
            (ensemble.at[pl.ds(pl.multiple_of(other * 32, 32), 32)], held_rows.at[block, rows]),
            (source, held_source.at[block, pl.ds(pl.multiple_of(half * 8, 8), 8)]),
            (wanted, held_wanted.at[space]),
        )

    def remote(origin, target, sends, receives, device):
        return pltpu.make_async_remote_copy(
            src_ref=origin,
            dst_ref=target,
            send_sem=sends,
            recv_sem=receives,
            device_id=device,
            device_id_type=pl.DeviceIdType.MESH,
        )

    across = lax.rem(space + HALF // 2, SPACE)

    def near_peer(step):
        block, half = halves(space)
        return {"space": half * (HALF // 2) + lax.rem(block + step, HALF // 2)}

    def shared_refs():
        block, half = halves(space)
        for sender, side_of in ((space, half), (across, 1 - half)):
            yield (
                held_source.at[block, pl.ds(pl.multiple_of(side_of * 8, 8), 8)],
                held_wanted.at[sender],
            )

    def relays():
        return [
            remote(origin, target, relay_send.at[kind], relay_recv.at[kind], {"space": across})
            for kind, (origin, target) in enumerate(piece_refs(space)[1:])
        ]

    def send_sums(turn, norm, product):
        norm = norm + pltpu.roll(norm, 64, 1)
        product = product + pltpu.roll(product, 64, 1)
        both = jnp.where(lane < 64, norm, product)
        tiles[turn, member] = both[:4] + both[4:]
        for step in range(1, TEAM):
            tile_copy(turn, step).start()

    def sums_here(turn):
        wait_bytes(tiles.at[turn, pl.ds(0, TEAM - 1)], tile_recv.at[turn])
        both = jnp.sum(tiles[turn], axis=0)
        both = jnp.concatenate([both, both])
        norm = jnp.sum(jnp.where(lane < 64, both, 0.0), axis=1, keepdims=True)
        product = jnp.sum(jnp.where(lane < 64, 0.0, both), axis=1, keepdims=True)
        return jnp.broadcast_to(norm, plane), jnp.broadcast_to(product, plane)

    def over_rows(body, start):
        def several(block, carry):
            for k in range(2):
                carry = body(block, k, carry)
            return carry

        return lax.fori_loop(0, HALF // 2, several, start)

    barrier = pltpu.get_barrier_semaphore()
    for step in range(1, SPACE):
        pl.semaphore_signal(barrier, inc=1, device_id=space_peer(step)[1], device_id_type=pl.DeviceIdType.MESH)
    for step in range(1, TEAM):
        pl.semaphore_signal(barrier, inc=1, device_id=team_peer(step), device_id_type=pl.DeviceIdType.MESH)
    for peer in sum_peers()[1]:
        for step in range(1, WIDE):
            pl.semaphore_signal(barrier, inc=1, device_id=peer(step)[1], device_id_type=pl.DeviceIdType.MESH)
    own = [
        pltpu.make_async_copy(origin, target, own_sems.at[kind])
        for kind, (origin, target) in enumerate(piece_refs(space))
    ]
    for copy in own:
        copy.start()
    pl.semaphore_wait(barrier, TEAM - 1 + SPACE - 1 + 3 * (WIDE - 1))
    for copy in relays():
        copy.start()
    for step in range(1, SPACE):
        other, device = space_peer(step)
        remote(*piece_refs(other)[0], swap_send.at[0], swap_recv.at[0], device).start()
    mine, theirs = shared_refs()
    for step in range(1, HALF // 2):
        for kind, target in enumerate(mine):
            origin = (source, wanted)[kind]
            remote(origin, target, swap_send.at[1 + kind], swap_recv.at[1 + kind], near_peer(step)).start()
    for copy in relays():
        copy.wait_recv()
    for step in range(1, HALF // 2):
        for kind, target in enumerate(theirs):
            remote(target, target, swap_send.at[1 + kind], swap_recv.at[1 + kind], near_peer(step)).start()

    @pl.when(member == 0)
    def _():
        source_edge[0] = jnp.zeros(source_edge.shape[1:], jnp.float32)
        for kind in range(ITERS - 1):
            edges[kind, 0] = jnp.zeros(edges.shape[2:], jnp.float32)

    @pl.when(member == TEAM - 1)
    def _():
        source_edge[1] = jnp.zeros(source_edge.shape[1:], jnp.float32)
        for kind in range(ITERS - 1):
            edges[kind, 1] = jnp.zeros(edges.shape[2:], jnp.float32)

    for copy in own:
        copy.wait()
    others = SPACE - 1
    wait_bytes(ensemble.at[pl.ds(0, others * 32)], swap_recv.at[0])
    wait_bytes(ensemble.at[pl.ds(0, (others - 1) * 8)], swap_recv.at[1])
    wait_bytes(held_wanted.at[pl.ds(0, others - 1)], swap_recv.at[2])

    def two_rows(lower, upper):
        return jnp.where(low_half, jnp.broadcast_to(lower, plane), jnp.broadcast_to(upper, plane))

    def close_ends(padded, outside):
        for y in range(4):
            first, last = padded[y, 1], padded[y, HALF]
            below = first if outside is None else outside
            above = last if outside is None else outside
            padded[y, 0] = jnp.where(low_half, below, pltpu.roll(last, 4, 0))
            padded[y, HALF + 1] = jnp.where(low_half, pltpu.roll(first, 4, 0), above)

    def begin(block, carry):
        rows = held_source[block]
        for k in range(2):
            for y in range(4):
                at = 4 * k + y
                held = held_rows[block, pl.ds(at, 8, stride=8), :]
                cond[y, 2 * block + k + 1] = jnp.exp(held)
                searched[y, 2 * block + k + 1] = two_rows(rows[at : at + 1], rows[8 + at : 9 + at])
        for upward in range(2):
            at = 3 * upward
            side[upward, block] = jnp.concatenate([rows[at + k : at + k + 1] for k in (0, 8, 4, 12)])
        return carry

    lax.fori_loop(0, HALF // 2, begin, 0)
    send_edges(COND)
    send_edges(SOURCE)
    close_ends(cond, None)
    close_ends(searched, jnp.zeros(plane, jnp.float32))

    @pl.when(member == 0)
    def _():
        cond_edge[0] = cond[0, pl.ds(1, HALF)]

    @pl.when(member == TEAM - 1)
    def _():
        cond_edge[1] = cond[3, pl.ds(1, HALF)]

    def inner_faces(block, k, carry):
        row = 2 * block + k
        here = cond[:, row + 1]
        face_x[:, row + 1] = harmonic(here, cond[:, row + 2])
        above = jnp.where(lane_4 == 127, here, pltpu.roll(here, 127, 2))
        upper = harmonic(here, above)
        face_z[:, row] = upper
        lower_z[:, row] = jnp.where(lane_4 == 0, here, pltpu.roll(upper, 1, 2))
        face_y[1:4, row] = harmonic(here[:3], here[1:])
        face_y[0, row] = here[0]
        face_y[4, row] = here[3]
        return carry

    over_rows(inner_faces, 0)
    for y in range(4):
        face_x[y, 0] = harmonic(cond[y, 0], cond[y, 1])

    def outer_faces(block, k, carry):
        row = 2 * block + k
        face_y[0, row] = harmonic(cond_edge[0, row], cond[0, row + 1])
        face_y[4, row] = harmonic(cond[3, row + 1], cond_edge[1, row])
        return carry

    def operate():
        def body(block, k, carry):
            row = 2 * block + k
            here = searched[:, row + 1]
            before = jnp.concatenate([here[:1], here[:3]])
            after = jnp.concatenate([here[1:], here[3:]])
            result = face_x[:, row + 1] * (here - searched[:, row + 2])
            result = result + face_x[:, row] * (here - searched[:, row])
            result = result + face_y[1:5, row] * (here - after)
            result = result + face_y[0:4, row] * (here - before)
            above = jnp.where(lane_4 == 127, 0.0, pltpu.roll(here, 127, 2))
            below = jnp.where(lane_4 == 0, 0.0, pltpu.roll(here, 1, 2))
            result = result + face_z[:, row] * (here - above)
            image[:, row] = result + lower_z[:, row] * (here - below)
            return carry

        over_rows(body, 0)

    def operate_edges(lower_edge, upper_edge):
        def body(block, k, carry):
            row = 2 * block + k
            image[0, row] = image[0, row] + face_y[0, row] * (searched[0, row + 1] - lower_edge(block, k))
            image[3, row] = image[3, row] + face_y[4, row] * (searched[3, row + 1] - upper_edge(block, k))
            return carry

        over_rows(body, 0)

    def over_planes(body, kind):
        def outer(block, k, carry):
            return body(slice(3, 4), 2 * block + k, body(slice(0, 1), 2 * block + k, carry))

        def inner(block, k, carry):
            return body(slice(1, 3), 2 * block + k, carry)

        sums = over_rows(outer, (zeros, zeros))
        if kind < ITERS - 1:
            send_edges(kind)
        return over_rows(inner, sums)

    zeros = jnp.zeros(plane, jnp.float32)
    operate()
    edges_here(COND)
    over_rows(outer_faces, 0)
    edges_here(SOURCE)

    def source_side(upward):
        def rows(block, k):
            four = source_edge[upward, block]
            return two_rows(four[2 * k : 2 * k + 1], four[2 * k + 1 : 2 * k + 2])

        return rows

    operate_edges(source_side(0), source_side(1))

    def first_sums(ys, row, carry):
        norm, product = carry
        image_here = image[ys, row]
        residual_here = searched[ys, row + 1]
        residual[ys, row] = residual_here
        searched[ys, row + 1] = image_here
        return norm + jnp.sum(residual_here * residual_here, axis=0), product + jnp.sum(
            residual_here * image_here, axis=0
        )

    norm, product = over_planes(first_sums, 0)

    norm_before = step_before = None
    for turn in range(ITERS):
        last = turn == ITERS - 1
        send_sums(turn, norm, product)
        if not last:
            close_ends(searched, zeros)
            operate()
            edges_here(turn)
            operate_edges(
                lambda block, k: edges[turn, 0, 2 * block + k], lambda block, k: edges[turn, 1, 2 * block + k]
            )
        norm_now, product_now = sums_here(turn)
        if turn == 0:
            step_size = norm_now / product_now
        else:
            ratio = norm_now / norm_before
            step_size = norm_now / (product_now - ratio * norm_now / step_before)
        norm_before, step_before = norm_now, step_size

        def update(ys, row, carry):
            norm, product = carry
            residual_here, image_here = residual[ys, row], searched[ys, row + 1]
            direction_here, along_here, beyond_here = residual_here, image_here, image[ys, row]
            answer_here = step_size * direction_here
            if turn > 0:
                direction_here = direction_here + ratio * direction[ys, row]
                along_here = along_here + ratio * along[ys, row]
                beyond_here = beyond_here + ratio * beyond[ys, row]
                answer_here = answer[ys, row] + step_size * direction_here
            residual_here = residual_here - step_size * along_here
            image_here = image_here - step_size * beyond_here
            answer[ys, row] = answer_here
            direction[ys, row] = direction_here
            along[ys, row] = along_here
            beyond[ys, row] = beyond_here
            residual[ys, row] = residual_here
            searched[ys, row + 1] = image_here
            return norm + jnp.sum(residual_here * residual_here, axis=0), product + jnp.sum(
                residual_here * image_here, axis=0
            )

        def finish(block, k, carry):
            row = 2 * block + k
            answer[:, row] = answer[:, row] + step_size * (residual[:, row] + ratio * direction[:, row])
            return carry

        if last:
            over_rows(finish, 0)
        else:
            edges_sent(turn)
            norm, product = over_planes(update, turn + 1)

    for block in range(HALF // 2):
        chosen = two_rows(held_wanted[block], held_wanted[HALF // 2 + block])
        value = zeros
        for choice in range(8):
            value = value + jnp.where(chosen == choice, answer[choice % 4, 2 * block + choice // 4], 0.0)
        picked[block] = value[:4]
        picked[HALF // 2 + block] = value[4:]

    returned[space] = picked[space]
    for step in range(1, SPACE):
        other, device = space_peer(step)
        pltpu.make_async_remote_copy(
            src_ref=picked.at[other],
            dst_ref=returned.at[space],
            send_sem=swap_send.at[3],
            recv_sem=swap_recv.at[3],
            device_id=device,
            device_id_type=pl.DeviceIdType.MESH,
        ).start()
    wait_bytes(returned.at[pl.ds(0, others)], swap_recv.at[3])
    for i in range(SPACE // 2):
        predicted[pl.ds(8 * i, 8)] = jnp.concatenate([returned[2 * i], returned[2 * i + 1]])

    values = predicted[...]
    inverse_sigma = 1.0 / jnp.sqrt(obs_var[...])
    spread = (values - jnp.mean(values, axis=0, keepdims=True)) * inverse_sigma
    misfit = (obs_values[...] - values) * inverse_sigma + obs_noise[...]
    for i, other in enumerate((spread, misfit)):
        product = lax.dot_general(
            spread, other, (((1,), (1,)), ((), ())), precision=lax.Precision.HIGHEST, preferred_element_type=jnp.float32
        )
        for j in range(HALF):
            part[HALF * i + j] = product[4 * j : 4 * j + 4]
    sum_everywhere(part, total, *sum_refs)

    edges_sent(COND)
    edges_sent(SOURCE)
    for turn in range(ITERS):
        wait_bytes(tiles.at[turn, pl.ds(0, TEAM - 1)], tile_send.at[turn])
    wait_bytes(ensemble.at[pl.ds(0, others * 32)], swap_send.at[0])
    wait_bytes(ensemble.at[pl.ds(0, (others - 1) * 8)], swap_send.at[1])
    wait_bytes(held_wanted.at[pl.ds(0, others - 1)], swap_send.at[2])
    wait_bytes(returned.at[pl.ds(0, others)], swap_send.at[3])
    for copy in relays():
        copy.wait_send()


def predict(ensemble, source, wanted, obs_values, obs_noise, obs_var):
    held = (4, HALF, 8, 128)
    padded = (4, HALF + 2, 8, 128)
    vmem = lambda *shape: pltpu.VMEM(shape, jnp.float32)
    return pl.pallas_call(
        conjugate_kernel,
        out_shape=[jax.ShapeDtypeStruct((rows, 128), jnp.float32) for rows in (128, 256)],
        in_specs=[pl.BlockSpec(memory_space=pl.ANY), *[pl.BlockSpec(memory_space=pltpu.VMEM)] * 5],
        out_specs=[pl.BlockSpec(memory_space=pltpu.VMEM)] * 2,
        scratch_shapes=[
            vmem(HALF // 2, 64, 128),
            vmem(HALF // 2, 16, 128),
            pltpu.VMEM((SPACE, 1, 128), jnp.int32),
            vmem(SPACE, 4, 128),
            vmem(SPACE, 4, 128),
            vmem(2, HALF // 2, 4, 128),
            vmem(*padded),
            vmem(4, HALF + 1, 8, 128),
            vmem(5, HALF, 8, 128),
            vmem(*held),
            vmem(*held),
            vmem(*padded),
            *[vmem(*held)] * 6,
            vmem(2, HALF, 8, 128),
            vmem(2, HALF // 2, 4, 128),
            vmem(ITERS - 1, 2, HALF, 8, 128),
            vmem(ITERS, TEAM, 4, 128),
            pltpu.SemaphoreType.DMA((ITERS + 1, 2)),
            pltpu.SemaphoreType.DMA((ITERS + 1, 2)),
            pltpu.SemaphoreType.DMA((ITERS,)),
            pltpu.SemaphoreType.DMA((ITERS,)),
            pltpu.SemaphoreType.DMA((4,)),
            pltpu.SemaphoreType.DMA((4,)),
            pltpu.SemaphoreType.DMA((3,)),
            pltpu.SemaphoreType.DMA((2,)),
            pltpu.SemaphoreType.DMA((2,)),
            vmem(64, 4, 128),
            vmem(WIDE - 1, WIDE, 4, 128),
            vmem(WIDE, 4, 128),
            vmem(WIDE - 1, 4, 128),
            vmem(4, 128),
            vmem(WIDE, 4, 128),
            vmem(WIDE, 4, 128),
            vmem(WIDE, WIDE, 4, 128),
            pltpu.SemaphoreType.DMA((5, WIDE - 1)),
            pltpu.SemaphoreType.DMA((5, WIDE - 1)),
        ],
        compiler_params=pltpu.CompilerParams(collective_id=2, has_side_effects=True),
        name="predict",
    )(ensemble, source, wanted, obs_values, obs_noise, obs_var)


PANEL = 8


def solve_kernel(total, ensemble, updated, gram, cross, scaled, weights):
    plane = (PANEL, 128)
    count = gram.shape[0]
    sublane = lax.broadcasted_iota(jnp.int32, plane, 0)
    lane = lax.broadcasted_iota(jnp.int32, plane, 1)
    whole = functools.partial(lax.dot_general, precision=lax.Precision.HIGHEST, preferred_element_type=jnp.float32)

    def spread(row):
        return jnp.broadcast_to(row, plane)

    for low in range(0, count, PANEL):
        gram[low : low + PANEL] = total[low : low + PANEL] + jnp.where(lane == sublane + low, count - 1.0, 0.0)
    cross[...] = total[count:]

    for low in range(0, count, PANEL):
        rows_g, rows_c = gram[low : low + PANEL], cross[low : low + PANEL]
        columns = [spread(rows_g[:, low + j : low + j + 1]) for j in range(PANEL)]
        pivots = {(i, j): spread(columns[j][i : i + 1]) for j in range(PANEL) for i in range(j + 1)}
        inverse, factor = [], {}
        for k in range(PANEL):
            inverse.append(1.0 / pivots[k, k])
            for i in range(k + 1, PANEL):
                factor[i, k] = pivots[k, i] * inverse[k]
                for j in range(i, PANEL):
                    pivots[i, j] = pivots[i, j] - factor[i, k] * pivots[k, j]
        solved = []
        for rows in (rows_g, rows_c):
            lines = [spread(rows[i : i + 1]) for i in range(PANEL)]
            for k in range(PANEL):
                for i in range(k + 1, PANEL):
                    lines[i] = lines[i] - factor[i, k] * lines[k]
            lines = [line * inverse[i] for i, line in enumerate(lines)]
            for k in reversed(range(PANEL)):
                for i in range(k):
                    lines[i] = lines[i] - factor[k, i] * lines[k]
            joined = lines[0]
            for i in range(1, PANEL):
                joined = jnp.where(sublane == i, lines[i], joined)
            solved.append(joined)
        scaled[low : low + PANEL] = solved[0]
        weights[low : low + PANEL] = solved[1]
        after = low + PANEL
        if after < count:
            taken = rows_g.T
            gram[after:] = gram[after:] - whole(taken, solved[0], (((1,), (0,)), ((), ())))[after:]
            cross[after:] = cross[after:] - whole(taken, solved[1], (((1,), (0,)), ((), ())))[after:]

    for low in range(count - 2 * PANEL, -1, -PANEL):
        known = low + PANEL
        left = jnp.where(lane >= known, scaled[low : low + PANEL], 0.0)
        weights[low : low + PANEL] = weights[low : low + PANEL] - whole(left, weights[...], (((1,), (0,)), ((), ())))

    turned = weights[...].T
    for row in range(PANEL):
        picks = [pl.ds(row + 8 * PANEL * i, PANEL, stride=8) for i in range(count // PANEL)]
        fields = [ensemble[pick, :] for pick in picks]
        mean = jnp.sum(sum(fields), axis=0, keepdims=True) * (1.0 / count)
        change = whole(turned, jnp.concatenate([field - mean for field in fields]), (((1,), (0,)), ((), ())))
        for i, pick in enumerate(picks):
            updated[pick, :] = fields[i] + change[PANEL * i : PANEL * (i + 1)]


def solve_and_update(total, ensemble):
    square = pltpu.VMEM((total.shape[1], total.shape[1]), jnp.float32)
    return pl.pallas_call(
        solve_kernel,
        out_shape=jax.ShapeDtypeStruct(ensemble.shape, jnp.float32),
        in_specs=[pl.BlockSpec(memory_space=pltpu.VMEM)] * 2,
        out_specs=pl.BlockSpec(memory_space=pltpu.VMEM),
        scratch_shapes=[square] * 4,
        name="solve_and_update",
    )(total, ensemble)


def local(ensemble, source, obs_rows, obs_values, obs_noise, obs_var):
    layers = source.shape[-1]
    fields = ensemble.reshape(-1, layers)
    wanted = jnp.broadcast_to(obs_rows.reshape(1, 1), (1, layers))
    predicted, total = predict(
        fields,
        source.reshape(-1, layers),
        wanted,
        obs_values.reshape(1, layers),
        obs_noise.reshape(-1, layers),
        obs_var.reshape(1, layers),
    )
    updated = solve_and_update(total, fields)
    return (updated.reshape(ensemble.shape), predicted.reshape(obs_noise.shape))


def solution(mesh):
    in_specs = (
        P(None, "space", "member", None),
        P("space", "member", None),
        P("space", "member", None),
        P("space", "member", None),
        P(None, "space", "member", None),
        P("space", "member", None),
    )
    out_specs = (P(None, "space", "member", None), P(None, "space", "member", None))
    return jax.shard_map(local, mesh=mesh, in_specs=in_specs, out_specs=out_specs, check_vma=False)
```

```python
import functools

import jax
import jax.numpy as jnp
from jax import lax
from jax.experimental import pallas as pl
from jax.experimental.pallas import tpu as pltpu
from jax.sharding import PartitionSpec as P

X, Y_LO, Y_HI, Z, CORES = 4, 4, 2, 8, 2
WIDE = 8

ITERS = 4


def place():
    member = lax.axis_index("member")
    space = lax.axis_index("space")
    x = lax.rem(member, X)
    y = lax.div(space, Z * CORES) * Y_LO + lax.div(member, X)
    z = lax.rem(lax.div(space, CORES), Z)
    return x, y, z, lax.rem(space, CORES)


def device_at(x, y, z, core):
    member = lax.rem(y, Y_LO) * X + x
    space = (lax.div(y, Y_LO) * Z + z) * CORES + core
    return {"member": member, "space": space}


def sum_peers():
    x, y, z, core = place()
    row = x * CORES + core

    def row_peer(step):
        other = lax.rem(row + step, WIDE)
        return other, device_at(lax.div(other, CORES), y, z, lax.rem(other, CORES))

    def y_peer(step):
        other = lax.rem(y + step, WIDE)
        return other, device_at(x, other, z, core)

    def z_peer(step):
        other = lax.rem(z + step, WIDE)
        return other, device_at(x, y, other, core)

    return (row, y, z), (row_peer, y_peer, z_peer)


def sum_everywhere(part, total, got_row, sum_row, got_y, sum_y, got_z, all_y, all_row, send_sems, recv_sems):
    (row, y, z), (row_peer, y_peer, z_peer) = sum_peers()

    def exchange(phase, peer, source, target):
        copies = []
        for step in range(1, WIDE):
            other, device = peer(step)
            copy = pltpu.make_async_remote_copy(
                src_ref=source(other),
                dst_ref=target(step),
                send_sem=send_sems.at[phase, step - 1],
                recv_sem=recv_sems.at[phase, step - 1],
                device_id=device,
                device_id_type=pl.DeviceIdType.MESH,
            )
            copy.start()
            copies.append(copy)
        return copies

    def arrived(copies):
        for copy in copies:
            copy.wait_recv()

    sent = []
    copies = exchange(0, row_peer, lambda o: part.at[pl.ds(o * WIDE, WIDE)], lambda s: got_row.at[s - 1])
    sent += copies
    arrived(copies)
    sum_row[...] = part[pl.ds(row * WIDE, WIDE)] + jnp.sum(got_row[...], axis=0)

    copies = exchange(1, y_peer, lambda o: sum_row.at[o], lambda s: got_y.at[s - 1])
    sent += copies
    arrived(copies)
    sum_y[...] = sum_row[y] + jnp.sum(got_y[...], axis=0)

    got_z[z] = sum_y[...]
    copies = exchange(2, z_peer, lambda o: sum_y, lambda s: got_z.at[z])
    sent += copies
    arrived(copies)
    sum_y_z = jnp.sum(got_z[...], axis=0)
    all_y[y] = sum_y_z

    copies = exchange(3, y_peer, lambda o: all_y.at[y], lambda s: all_y.at[y])
    sent += copies
    arrived(copies)

    copies = exchange(4, row_peer, lambda o: all_y, lambda s: all_row.at[row])
    sent += copies
    all_row[row] = all_y[...]
    arrived(copies)
    for i in range(WIDE):
        for j in range(0, WIDE, 2):
            total[pl.ds(4 * (WIDE * i + j), 8)] = jnp.concatenate([all_row[i, j], all_row[i, j + 1]])
    for copy in sent:
        copy.wait_send()


def harmonic(first_cond, second_cond):
    return 2.0 * first_cond * second_cond / (first_cond + second_cond)


HALF = 32
TEAM = 16
SPACE = 32
COND, SOURCE = ITERS - 1, ITERS


def conjugate_kernel(
    ensemble,
    source,
    obs_row,
    obs_values,
    obs_noise,
    obs_var,
    predicted,
    total,
    wanted,
    held_rows,
    held_source,
    held_wanted,
    picked,
    returned,
    side,
    cond,
    face_x,
    face_y,
    face_z,
    lower_z,
    searched,
    image,
    residual,
    direction,
    along,
    beyond,
    answer,
    cond_edge,
    source_edge,
    edges,
    tiles,
    edge_send,
    edge_recv,
    tile_send,
    tile_recv,
    swap_send,
    swap_recv,
    own_sems,
    relay_send,
    relay_recv,
    part,
    *sum_refs,
):
    member = lax.axis_index("member")
    space = lax.axis_index("space")
    plane = (8, 128)
    sublane = lax.broadcasted_iota(jnp.int32, plane, 0)
    lane = lax.broadcasted_iota(jnp.int32, plane, 1)
    lane_4 = lax.broadcasted_iota(jnp.int32, (4, 8, 128), 2)
    low_half = sublane < 4

    def team_peer(step):
        return {"member": lax.rem(member + step, TEAM)}

    def edge_copy(kind, upward):
        if kind == COND:
            origin, target = cond.at[3 * upward, pl.ds(1, HALF)], cond_edge.at[1 - upward]
        elif kind == SOURCE:
            origin, target = side.at[upward], source_edge.at[1 - upward]
        else:
            origin, target = searched.at[3 * upward, pl.ds(1, HALF)], edges.at[kind, 1 - upward]
        return pltpu.make_async_remote_copy(
            src_ref=origin,
            dst_ref=target,
            send_sem=edge_send.at[kind, upward],
            recv_sem=edge_recv.at[kind, 1 - upward],
            device_id=team_peer(1 if upward else TEAM - 1),
            device_id_type=pl.DeviceIdType.MESH,
        )

    def send_edges(kind):
        @pl.when(member > 0)
        def _():
            edge_copy(kind, 0).start()

        @pl.when(member < TEAM - 1)
        def _():
            edge_copy(kind, 1).start()

    def edges_sent(kind):
        @pl.when(member > 0)
        def _():
            edge_copy(kind, 0).wait_send()

        @pl.when(member < TEAM - 1)
        def _():
            edge_copy(kind, 1).wait_send()

    def edges_here(kind):
        @pl.when(member > 0)
        def _():
            edge_copy(kind, 1).wait_recv()

        @pl.when(member < TEAM - 1)
        def _():
            edge_copy(kind, 0).wait_recv()

    def tile_copy(turn, step):
        return pltpu.make_async_remote_copy(
            src_ref=tiles.at[turn, member],
            dst_ref=tiles.at[turn, member],
            send_sem=tile_send.at[turn],
            recv_sem=tile_recv.at[turn],
            device_id=team_peer(step),
            device_id_type=pl.DeviceIdType.MESH,
        )

    def wait_bytes(ref, sem):
        pltpu.make_async_copy(ref, ref, sem).wait()

    def space_peer(step):
        other = lax.rem(space + step, SPACE)
        return other, {"space": other}

    def halves(index):
        return lax.rem(index, HALF // 2), lax.div(index, HALF // 2)

    def piece_refs(other):
        block, half = halves(space)
        rows = pl.ds(pl.multiple_of(half * 32, 32), 32)
        return (
            (ensemble.at[pl.ds(pl.multiple_of(other * 32, 32), 32)], held_rows.at[block, rows]),
            (source, held_source.at[block, pl.ds(pl.multiple_of(half * 8, 8), 8)]),
            (wanted, held_wanted.at[space]),
        )

    def remote(origin, target, sends, receives, device):
        return pltpu.make_async_remote_copy(
            src_ref=origin,
            dst_ref=target,
            send_sem=sends,
            recv_sem=receives,
            device_id=device,
            device_id_type=pl.DeviceIdType.MESH,
        )

    across = lax.rem(space + HALF // 2, SPACE)

    def near_peer(step):
        block, half = halves(space)
        return {"space": half * (HALF // 2) + lax.rem(block + step, HALF // 2)}

    def shared_refs():
        block, half = halves(space)
        for sender, side_of in ((space, half), (across, 1 - half)):
            yield (
                held_source.at[block, pl.ds(pl.multiple_of(side_of * 8, 8), 8)],
                held_wanted.at[sender],
            )

    def relays():
        return [
            remote(origin, target, relay_send.at[kind], relay_recv.at[kind], {"space": across})
            for kind, (origin, target) in enumerate(piece_refs(space)[1:])
        ]

    def send_sums(turn, norm, product):
        norm = norm + pltpu.roll(norm, 64, 1)
        product = product + pltpu.roll(product, 64, 1)
        both = jnp.where(lane < 64, norm, product)
        tiles[turn, member] = both[:4] + both[4:]
        for step in range(1, TEAM):
            tile_copy(turn, step).start()

    def sums_here(turn):
        wait_bytes(tiles.at[turn, pl.ds(0, TEAM - 1)], tile_recv.at[turn])
        both = jnp.sum(tiles[turn], axis=0)
        both = jnp.concatenate([both, both])
        norm = jnp.sum(jnp.where(lane < 64, both, 0.0), axis=1, keepdims=True)
        product = jnp.sum(jnp.where(lane < 64, 0.0, both), axis=1, keepdims=True)
        return jnp.broadcast_to(norm, plane), jnp.broadcast_to(product, plane)

    def over_rows(body, start):
        def several(block, carry):
            for k in range(2):
                carry = body(block, k, carry)
            return carry

        return lax.fori_loop(0, HALF // 2, several, start)

    wanted[...] = jnp.broadcast_to(obs_row[...], wanted.shape)
    barrier = pltpu.get_barrier_semaphore()
    for step in range(1, SPACE):
        pl.semaphore_signal(barrier, inc=1, device_id=space_peer(step)[1], device_id_type=pl.DeviceIdType.MESH)
    for step in range(1, TEAM):
        pl.semaphore_signal(barrier, inc=1, device_id=team_peer(step), device_id_type=pl.DeviceIdType.MESH)
    for peer in sum_peers()[1]:
        for step in range(1, WIDE):
            pl.semaphore_signal(barrier, inc=1, device_id=peer(step)[1], device_id_type=pl.DeviceIdType.MESH)
    own = [
        pltpu.make_async_copy(origin, target, own_sems.at[kind])
        for kind, (origin, target) in enumerate(piece_refs(space))
    ]
    for copy in own:
        copy.start()
    pl.semaphore_wait(barrier, TEAM - 1 + SPACE - 1 + 3 * (WIDE - 1))
    for copy in relays():
        copy.start()
    for step in range(1, SPACE):
        other, device = space_peer(step)
        remote(*piece_refs(other)[0], swap_send.at[0], swap_recv.at[0], device).start()
    mine, theirs = shared_refs()
    for step in range(1, HALF // 2):
        for kind, target in enumerate(mine):
            origin = (source, wanted)[kind]
            remote(origin, target, swap_send.at[1 + kind], swap_recv.at[1 + kind], near_peer(step)).start()
    for copy in relays():
        copy.wait_recv()
    for step in range(1, HALF // 2):
        for kind, target in enumerate(theirs):
            remote(target, target, swap_send.at[1 + kind], swap_recv.at[1 + kind], near_peer(step)).start()

    @pl.when(member == 0)
    def _():
        source_edge[0] = jnp.zeros(source_edge.shape[1:], jnp.float32)
        for kind in range(ITERS - 1):
            edges[kind, 0] = jnp.zeros(edges.shape[2:], jnp.float32)

    @pl.when(member == TEAM - 1)
    def _():
        source_edge[1] = jnp.zeros(source_edge.shape[1:], jnp.float32)
        for kind in range(ITERS - 1):
            edges[kind, 1] = jnp.zeros(edges.shape[2:], jnp.float32)

    for copy in own:
        copy.wait()
    others = SPACE - 1
    wait_bytes(ensemble.at[pl.ds(0, others * 32)], swap_recv.at[0])
    wait_bytes(ensemble.at[pl.ds(0, (others - 1) * 8)], swap_recv.at[1])
    wait_bytes(held_wanted.at[pl.ds(0, others - 1)], swap_recv.at[2])

    def two_rows(lower, upper):
        return jnp.where(low_half, jnp.broadcast_to(lower, plane), jnp.broadcast_to(upper, plane))

    def close_ends(padded, outside):
        for y in range(4):
            first, last = padded[y, 1], padded[y, HALF]
            below = first if outside is None else outside
            above = last if outside is None else outside
            padded[y, 0] = jnp.where(low_half, below, pltpu.roll(last, 4, 0))
            padded[y, HALF + 1] = jnp.where(low_half, pltpu.roll(first, 4, 0), above)

    def begin(block, carry):
        rows = held_source[block]
        for k in range(2):
            for y in range(4):
                at = 4 * k + y
                held = held_rows[block, pl.ds(at, 8, stride=8), :]
                cond[y, 2 * block + k + 1] = jnp.exp(held)
                searched[y, 2 * block + k + 1] = two_rows(rows[at : at + 1], rows[8 + at : 9 + at])
        for upward in range(2):
            at = 3 * upward
            side[upward, block] = jnp.concatenate([rows[at + k : at + k + 1] for k in (0, 8, 4, 12)])
        return carry

    lax.fori_loop(0, HALF // 2, begin, 0)
    send_edges(COND)
    send_edges(SOURCE)
    close_ends(cond, None)
    close_ends(searched, jnp.zeros(plane, jnp.float32))

    @pl.when(member == 0)
    def _():
        cond_edge[0] = cond[0, pl.ds(1, HALF)]

    @pl.when(member == TEAM - 1)
    def _():
        cond_edge[1] = cond[3, pl.ds(1, HALF)]

    def inner_faces(block, k, carry):
        row = 2 * block + k
        here = cond[:, row + 1]
        face_x[:, row + 1] = harmonic(here, cond[:, row + 2])
        above = jnp.where(lane_4 == 127, here, pltpu.roll(here, 127, 2))
        upper = harmonic(here, above)
        face_z[:, row] = upper
        lower_z[:, row] = jnp.where(lane_4 == 0, here, pltpu.roll(upper, 1, 2))
        face_y[1:4, row] = harmonic(here[:3], here[1:])
        face_y[0, row] = here[0]
        face_y[4, row] = here[3]
        return carry

    over_rows(inner_faces, 0)
    for y in range(4):
        face_x[y, 0] = harmonic(cond[y, 0], cond[y, 1])

    def outer_faces(block, k, carry):
        row = 2 * block + k
        face_y[0, row] = harmonic(cond_edge[0, row], cond[0, row + 1])
        face_y[4, row] = harmonic(cond[3, row + 1], cond_edge[1, row])
        return carry

    def operate():
        def body(block, k, carry):
            row = 2 * block + k
            here = searched[:, row + 1]
            before = jnp.concatenate([here[:1], here[:3]])
            after = jnp.concatenate([here[1:], here[3:]])
            result = face_x[:, row + 1] * (here - searched[:, row + 2])
            result = result + face_x[:, row] * (here - searched[:, row])
            result = result + face_y[1:5, row] * (here - after)
            result = result + face_y[0:4, row] * (here - before)
            above = jnp.where(lane_4 == 127, 0.0, pltpu.roll(here, 127, 2))
            below = jnp.where(lane_4 == 0, 0.0, pltpu.roll(here, 1, 2))
            result = result + face_z[:, row] * (here - above)
            image[:, row] = result + lower_z[:, row] * (here - below)
            return carry

        over_rows(body, 0)

    def operate_edges(lower_edge, upper_edge):
        def body(block, k, carry):
            row = 2 * block + k
            image[0, row] = image[0, row] + face_y[0, row] * (searched[0, row + 1] - lower_edge(block, k))
            image[3, row] = image[3, row] + face_y[4, row] * (searched[3, row + 1] - upper_edge(block, k))
            return carry

        over_rows(body, 0)

    def over_planes(body, kind):
        def outer(block, k, carry):
            return body(slice(3, 4), 2 * block + k, body(slice(0, 1), 2 * block + k, carry))

        def inner(block, k, carry):
            return body(slice(1, 3), 2 * block + k, carry)

        sums = over_rows(outer, (zeros, zeros))
        if kind < ITERS - 1:
            send_edges(kind)
        return over_rows(inner, sums)

    zeros = jnp.zeros(plane, jnp.float32)
    operate()
    edges_here(COND)
    over_rows(outer_faces, 0)
    edges_here(SOURCE)

    def source_side(upward):
        def rows(block, k):
            four = source_edge[upward, block]
            return two_rows(four[2 * k : 2 * k + 1], four[2 * k + 1 : 2 * k + 2])

        return rows

    operate_edges(source_side(0), source_side(1))

    def first_sums(ys, row, carry):
        norm, product = carry
        image_here = image[ys, row]
        residual_here = searched[ys, row + 1]
        residual[ys, row] = residual_here
        searched[ys, row + 1] = image_here
        return norm + jnp.sum(residual_here * residual_here, axis=0), product + jnp.sum(
            residual_here * image_here, axis=0
        )

    norm, product = over_planes(first_sums, 0)

    norm_before = step_before = None
    for turn in range(ITERS):
        last = turn == ITERS - 1
        send_sums(turn, norm, product)
        if not last:
            close_ends(searched, zeros)
            operate()
            edges_here(turn)
            operate_edges(
                lambda block, k: edges[turn, 0, 2 * block + k], lambda block, k: edges[turn, 1, 2 * block + k]
            )
        norm_now, product_now = sums_here(turn)
        if turn == 0:
            step_size = norm_now / product_now
        else:
            ratio = norm_now / norm_before
            step_size = norm_now / (product_now - ratio * norm_now / step_before)
        norm_before, step_before = norm_now, step_size

        def update(ys, row, carry):
            norm, product = carry
            residual_here, image_here = residual[ys, row], searched[ys, row + 1]
            direction_here, along_here, beyond_here = residual_here, image_here, image[ys, row]
            answer_here = step_size * direction_here
            if turn > 0:
                direction_here = direction_here + ratio * direction[ys, row]
                along_here = along_here + ratio * along[ys, row]
                beyond_here = beyond_here + ratio * beyond[ys, row]
                answer_here = answer[ys, row] + step_size * direction_here
            residual_here = residual_here - step_size * along_here
            image_here = image_here - step_size * beyond_here
            answer[ys, row] = answer_here
            direction[ys, row] = direction_here
            along[ys, row] = along_here
            beyond[ys, row] = beyond_here
            residual[ys, row] = residual_here
            searched[ys, row + 1] = image_here
            return norm + jnp.sum(residual_here * residual_here, axis=0), product + jnp.sum(
                residual_here * image_here, axis=0
            )

        def finish(block, k, carry):
            row = 2 * block + k
            answer[:, row] = answer[:, row] + step_size * (residual[:, row] + ratio * direction[:, row])
            return carry

        if last:
            over_rows(finish, 0)
        else:
            edges_sent(turn)
            norm, product = over_planes(update, turn + 1)

    for block in range(HALF // 2):
        chosen = two_rows(held_wanted[block], held_wanted[HALF // 2 + block])
        value = zeros
        for choice in range(8):
            value = value + jnp.where(chosen == choice, answer[choice % 4, 2 * block + choice // 4], 0.0)
        picked[block] = value[:4]
        picked[HALF // 2 + block] = value[4:]

    returned[space] = picked[space]
    for step in range(1, SPACE):
        other, device = space_peer(step)
        pltpu.make_async_remote_copy(
            src_ref=picked.at[other],
            dst_ref=returned.at[space],
            send_sem=swap_send.at[3],
            recv_sem=swap_recv.at[3],
            device_id=device,
            device_id_type=pl.DeviceIdType.MESH,
        ).start()
    wait_bytes(returned.at[pl.ds(0, others)], swap_recv.at[3])
    for i in range(SPACE // 2):
        predicted[pl.ds(8 * i, 8)] = jnp.concatenate([returned[2 * i], returned[2 * i + 1]])

    values = predicted[...]
    inverse_sigma = 1.0 / jnp.sqrt(obs_var[...])
    spread = (values - jnp.mean(values, axis=0, keepdims=True)) * inverse_sigma
    misfit = (obs_values[...] - values) * inverse_sigma + obs_noise[...]
    for i, other in enumerate((spread, misfit)):
        product = lax.dot_general(
            spread, other, (((1,), (1,)), ((), ())), precision=lax.Precision.HIGHEST, preferred_element_type=jnp.float32
        )
        for j in range(HALF):
            part[HALF * i + j] = product[4 * j : 4 * j + 4]
    sum_everywhere(part, total, *sum_refs)

    edges_sent(COND)
    edges_sent(SOURCE)
    for turn in range(ITERS):
        wait_bytes(tiles.at[turn, pl.ds(0, TEAM - 1)], tile_send.at[turn])
    wait_bytes(ensemble.at[pl.ds(0, others * 32)], swap_send.at[0])
    wait_bytes(ensemble.at[pl.ds(0, (others - 1) * 8)], swap_send.at[1])
    wait_bytes(held_wanted.at[pl.ds(0, others - 1)], swap_send.at[2])
    wait_bytes(returned.at[pl.ds(0, others)], swap_send.at[3])
    for copy in relays():
        copy.wait_send()


def predict(ensemble, source, obs_row, obs_values, obs_noise, obs_var):
    held = (4, HALF, 8, 128)
    padded = (4, HALF + 2, 8, 128)
    vmem = lambda *shape: pltpu.VMEM(shape, jnp.float32)
    return pl.pallas_call(
        conjugate_kernel,
        out_shape=[jax.ShapeDtypeStruct((rows, 128), jnp.float32) for rows in (128, 256)],
        in_specs=[pl.BlockSpec(memory_space=pl.ANY), *[pl.BlockSpec(memory_space=pltpu.VMEM)] * 5],
        out_specs=[pl.BlockSpec(memory_space=pltpu.VMEM)] * 2,
        scratch_shapes=[
            pltpu.VMEM((1, 128), jnp.int32),
            vmem(HALF // 2, 64, 128),
            vmem(HALF // 2, 16, 128),
            pltpu.VMEM((SPACE, 1, 128), jnp.int32),
            vmem(SPACE, 4, 128),
            vmem(SPACE, 4, 128),
            vmem(2, HALF // 2, 4, 128),
            vmem(*padded),
            vmem(4, HALF + 1, 8, 128),
            vmem(5, HALF, 8, 128),
            vmem(*held),
            vmem(*held),
            vmem(*padded),
            *[vmem(*held)] * 6,
            vmem(2, HALF, 8, 128),
            vmem(2, HALF // 2, 4, 128),
            vmem(ITERS - 1, 2, HALF, 8, 128),
            vmem(ITERS, TEAM, 4, 128),
            pltpu.SemaphoreType.DMA((ITERS + 1, 2)),
            pltpu.SemaphoreType.DMA((ITERS + 1, 2)),
            pltpu.SemaphoreType.DMA((ITERS,)),
            pltpu.SemaphoreType.DMA((ITERS,)),
            pltpu.SemaphoreType.DMA((4,)),
            pltpu.SemaphoreType.DMA((4,)),
            pltpu.SemaphoreType.DMA((3,)),
            pltpu.SemaphoreType.DMA((2,)),
            pltpu.SemaphoreType.DMA((2,)),
            vmem(64, 4, 128),
            vmem(WIDE - 1, WIDE, 4, 128),
            vmem(WIDE, 4, 128),
            vmem(WIDE - 1, 4, 128),
            vmem(4, 128),
            vmem(WIDE, 4, 128),
            vmem(WIDE, 4, 128),
            vmem(WIDE, WIDE, 4, 128),
            pltpu.SemaphoreType.DMA((5, WIDE - 1)),
            pltpu.SemaphoreType.DMA((5, WIDE - 1)),
        ],
        compiler_params=pltpu.CompilerParams(collective_id=2, has_side_effects=True),
        name="predict",
    )(ensemble, source, obs_row, obs_values, obs_noise, obs_var)


PANEL, GROUP = 8, 32


def solve_kernel(total, ensemble, values, updated, predicted, gram, cross, scaled, weights):
    plane = (PANEL, 128)
    count = gram.shape[0]
    sublane = lax.broadcasted_iota(jnp.int32, plane, 0)
    lane = lax.broadcasted_iota(jnp.int32, plane, 1)
    whole = functools.partial(lax.dot_general, precision=lax.Precision.HIGHEST, preferred_element_type=jnp.float32)

    def spread(row):
        return jnp.broadcast_to(row, plane)

    predicted[...] = values[...]
    for low in range(0, count, PANEL):
        gram[low : low + PANEL] = total[low : low + PANEL] + jnp.where(lane == sublane + low, count - 1.0, 0.0)
    cross[...] = total[count:]

    for low in range(0, count, PANEL):
        first = low - low % GROUP
        rows_g, rows_c = gram[low : low + PANEL], cross[low : low + PANEL]
        for k in range(first, low):
            if k % PANEL == 0:
                held = rows_g
            ahead = spread(held[:, k : k + 1])
            rows_g = rows_g - ahead * spread(scaled[k : k + 1])
            rows_c = rows_c - ahead * spread(weights[k : k + 1])
        gram[low : low + PANEL] = rows_g
        columns = [spread(rows_g[:, low + j : low + j + 1]) for j in range(PANEL)]
        pivots = {(i, j): spread(columns[j][i : i + 1]) for j in range(PANEL) for i in range(j + 1)}
        inverse, factor = [], {}
        for k in range(PANEL):
            inverse.append(1.0 / pivots[k, k])
            for i in range(k + 1, PANEL):
                factor[i, k] = pivots[k, i] * inverse[k]
                for j in range(i, PANEL):
                    pivots[i, j] = pivots[i, j] - factor[i, k] * pivots[k, j]
        solved = []
        for rows in (rows_g, rows_c):
            lines = [spread(rows[i : i + 1]) for i in range(PANEL)]
            for k in range(PANEL):
                for i in range(k + 1, PANEL):
                    lines[i] = lines[i] - factor[i, k] * lines[k]
            lines = [line * inverse[i] for i, line in enumerate(lines)]
            for k in reversed(range(PANEL)):
                for i in range(k):
                    lines[i] = lines[i] - factor[k, i] * lines[k]
            joined = lines[0]
            for i in range(1, PANEL):
                joined = jnp.where(sublane == i, lines[i], joined)
            solved.append(joined)
        scaled[low : low + PANEL] = solved[0]
        weights[low : low + PANEL] = solved[1]
        after = low + PANEL
        if after % GROUP == 0 and after < count:
            taken = gram[first:after].T
            for target, factors in ((gram, scaled), (cross, weights)):
                change = whole(taken, factors[first:after], (((1,), (0,)), ((), ())))
                target[after:] = target[after:] - change[after:]

    for first in range(count - GROUP, -1, -GROUP):
        group = slice(first, first + GROUP)
        if first + GROUP < count:
            later = lax.broadcasted_iota(jnp.int32, (GROUP, count), 1) >= first + GROUP
            left = jnp.where(later, scaled[group], 0.0)
            weights[group] = weights[group] - whole(left, weights[...], (((1,), (0,)), ((), ())))
        for low in range(first + GROUP - 2 * PANEL, first - 1, -PANEL):
            rows_g, rows_c = scaled[low : low + PANEL], weights[low : low + PANEL]
            for k in range(low + PANEL, first + GROUP):
                rows_c = rows_c - spread(rows_g[:, k : k + 1]) * spread(weights[k : k + 1])
            weights[low : low + PANEL] = rows_c

    turned = weights[...].T
    for row in range(PANEL):
        picks = [pl.ds(row + 8 * PANEL * i, PANEL, stride=8) for i in range(count // PANEL)]
        fields = [ensemble[pick, :] for pick in picks]
        mean = jnp.sum(sum(fields), axis=0, keepdims=True) * (1.0 / count)
        change = whole(turned, jnp.concatenate([field - mean for field in fields]), (((1,), (0,)), ((), ())))
        for i, pick in enumerate(picks):
            updated[pick, :] = fields[i] + change[PANEL * i : PANEL * (i + 1)]


def solve_and_update(total, ensemble, values):
    square = pltpu.VMEM((total.shape[1], total.shape[1]), jnp.float32)
    return pl.pallas_call(
        solve_kernel,
        out_shape=[jax.ShapeDtypeStruct(array.shape, jnp.float32) for array in (ensemble, values)],
        in_specs=[pl.BlockSpec(memory_space=pltpu.VMEM)] * 3,
        out_specs=[pl.BlockSpec(memory_space=pltpu.VMEM)] * 2,
        scratch_shapes=[square] * 4,
        name="solve_and_update",
    )(total, ensemble, values)


def local(ensemble, source, obs_rows, obs_values, obs_noise, obs_var):
    layers = source.shape[-1]
    fields = ensemble.reshape(-1, layers)
    predicted, total = predict(
        fields,
        source.reshape(-1, layers),
        obs_rows.reshape(1, 1),
        obs_values.reshape(1, layers),
        obs_noise.reshape(-1, layers),
        obs_var.reshape(1, layers),
    )
    updated, predicted = solve_and_update(total, fields, predicted)
    return (updated.reshape(ensemble.shape), predicted.reshape(obs_noise.shape))


def solution(mesh):
    in_specs = (
        P(None, "space", "member", None),
        P("space", "member", None),
        P("space", "member", None),
        P("space", "member", None),
        P(None, "space", "member", None),
        P("space", "member", None),
    )
    out_specs = (P(None, "space", "member", None), P(None, "space", "member", None))
    return jax.shard_map(local, mesh=mesh, in_specs=in_specs, out_specs=out_specs, check_vma=False)
```

```python
import functools

import jax
import jax.numpy as jnp
from jax import lax
from jax.experimental import pallas as pl
from jax.experimental.pallas import tpu as pltpu
from jax.sharding import PartitionSpec as P

X, Y_LO, Y_HI, Z, CORES = 4, 4, 2, 8, 2
WIDE = 8

ITERS = 4


def place():
    member = lax.axis_index("member")
    space = lax.axis_index("space")
    x = lax.rem(member, X)
    y = lax.div(space, Z * CORES) * Y_LO + lax.div(member, X)
    z = lax.rem(lax.div(space, CORES), Z)
    return x, y, z, lax.rem(space, CORES)


def device_at(x, y, z, core):
    member = lax.rem(y, Y_LO) * X + x
    space = (lax.div(y, Y_LO) * Z + z) * CORES + core
    return {"member": member, "space": space}


def sum_peers():
    x, y, z, core = place()
    row = x * CORES + core

    def row_peer(step):
        other = lax.rem(row + step, WIDE)
        return other, device_at(lax.div(other, CORES), y, z, lax.rem(other, CORES))

    def y_peer(step):
        other = lax.rem(y + step, WIDE)
        return other, device_at(x, other, z, core)

    def z_peer(step):
        other = lax.rem(z + step, WIDE)
        return other, device_at(x, y, other, core)

    return (row, y, z), (row_peer, y_peer, z_peer)


def sum_everywhere(part, total, got_row, sum_row, got_y, sum_y, got_z, all_y, all_row, send_sems, recv_sems):
    (row, y, z), (row_peer, y_peer, z_peer) = sum_peers()

    def exchange(phase, peer, source, target):
        copies = []
        for step in range(1, WIDE):
            other, device = peer(step)
            copy = pltpu.make_async_remote_copy(
                src_ref=source(other),
                dst_ref=target(step),
                send_sem=send_sems.at[phase, step - 1],
                recv_sem=recv_sems.at[phase, step - 1],
                device_id=device,
                device_id_type=pl.DeviceIdType.MESH,
            )
            copy.start()
            copies.append(copy)
        return copies

    def arrived(copies):
        for copy in copies:
            copy.wait_recv()

    sent = []
    copies = exchange(0, row_peer, lambda o: part.at[pl.ds(o * WIDE, WIDE)], lambda s: got_row.at[s - 1])
    sent += copies
    arrived(copies)
    sum_row[...] = part[pl.ds(row * WIDE, WIDE)] + jnp.sum(got_row[...], axis=0)

    copies = exchange(1, y_peer, lambda o: sum_row.at[o], lambda s: got_y.at[s - 1])
    sent += copies
    arrived(copies)
    sum_y[...] = sum_row[y] + jnp.sum(got_y[...], axis=0)

    got_z[z] = sum_y[...]
    copies = exchange(2, z_peer, lambda o: sum_y, lambda s: got_z.at[z])
    sent += copies
    arrived(copies)
    sum_y_z = jnp.sum(got_z[...], axis=0)
    all_y[y] = sum_y_z

    copies = exchange(3, y_peer, lambda o: all_y.at[y], lambda s: all_y.at[y])
    sent += copies
    arrived(copies)

    copies = exchange(4, row_peer, lambda o: all_y, lambda s: all_row.at[row])
    sent += copies
    all_row[row] = all_y[...]
    arrived(copies)
    for i in range(WIDE):
        for j in range(0, WIDE, 2):
            total[pl.ds(4 * (WIDE * i + j), 8)] = jnp.concatenate([all_row[i, j], all_row[i, j + 1]])
    for copy in sent:
        copy.wait_send()


def harmonic(first_cond, second_cond):
    return 2.0 * first_cond * second_cond / (first_cond + second_cond)


HALF = 32
TEAM = 16
SPACE = 32
COND, SOURCE = ITERS - 1, ITERS


def conjugate_kernel(
    ensemble,
    source,
    obs_row,
    obs_values,
    obs_noise,
    obs_var,
    predicted,
    total,
    wanted,
    held_rows,
    held_source,
    held_wanted,
    picked,
    returned,
    side,
    cond,
    face_x,
    face_y,
    face_z,
    lower_z,
    searched,
    image,
    residual,
    direction,
    along,
    beyond,
    answer,
    cond_edge,
    source_edge,
    edges,
    tiles,
    edge_send,
    edge_recv,
    tile_send,
    tile_recv,
    swap_send,
    swap_recv,
    own_sems,
    relay_send,
    relay_recv,
    part,
    *sum_refs,
):
    member = lax.axis_index("member")
    space = lax.axis_index("space")
    plane = (8, 128)
    sublane = lax.broadcasted_iota(jnp.int32, plane, 0)
    lane = lax.broadcasted_iota(jnp.int32, plane, 1)
    lane_4 = lax.broadcasted_iota(jnp.int32, (4, 8, 128), 2)
    low_half = sublane < 4

    def team_peer(step):
        return {"member": lax.rem(member + step, TEAM)}

    def edge_copy(kind, upward):
        if kind == COND:
            origin, target = cond.at[3 * upward, pl.ds(1, HALF)], cond_edge.at[1 - upward]
        elif kind == SOURCE:
            origin, target = side.at[upward], source_edge.at[1 - upward]
        else:
            origin, target = searched.at[3 * upward, pl.ds(1, HALF)], edges.at[kind, 1 - upward]
        return pltpu.make_async_remote_copy(
            src_ref=origin,
            dst_ref=target,
            send_sem=edge_send.at[kind, upward],
            recv_sem=edge_recv.at[kind, 1 - upward],
            device_id=team_peer(1 if upward else TEAM - 1),
            device_id_type=pl.DeviceIdType.MESH,
        )

    def send_edges(kind):
        @pl.when(member > 0)
        def _():
            edge_copy(kind, 0).start()

        @pl.when(member < TEAM - 1)
        def _():
            edge_copy(kind, 1).start()

    def edges_sent(kind):
        @pl.when(member > 0)
        def _():
            edge_copy(kind, 0).wait_send()

        @pl.when(member < TEAM - 1)
        def _():
            edge_copy(kind, 1).wait_send()

    def edges_here(kind):
        @pl.when(member > 0)
        def _():
            edge_copy(kind, 1).wait_recv()

        @pl.when(member < TEAM - 1)
        def _():
            edge_copy(kind, 0).wait_recv()

    def tile_copy(turn, step):
        return pltpu.make_async_remote_copy(
            src_ref=tiles.at[turn, member],
            dst_ref=tiles.at[turn, member],
            send_sem=tile_send.at[turn],
            recv_sem=tile_recv.at[turn],
            device_id=team_peer(step),
            device_id_type=pl.DeviceIdType.MESH,
        )

    def wait_bytes(ref, sem):
        pltpu.make_async_copy(ref, ref, sem).wait()

    def space_peer(step):
        other = lax.rem(space + step, SPACE)
        return other, {"space": other}

    def halves(index):
        return lax.rem(index, HALF // 2), lax.div(index, HALF // 2)

    def piece_refs(other):
        block, half = halves(space)
        rows = pl.ds(pl.multiple_of(half * 32, 32), 32)
        return (
            (ensemble.at[pl.ds(pl.multiple_of(other * 32, 32), 32)], held_rows.at[block, rows]),
            (source, held_source.at[block, pl.ds(pl.multiple_of(half * 8, 8), 8)]),
            (wanted, held_wanted.at[space]),
        )

    def remote(origin, target, sends, receives, device):
        return pltpu.make_async_remote_copy(
            src_ref=origin,
            dst_ref=target,
            send_sem=sends,
            recv_sem=receives,
            device_id=device,
            device_id_type=pl.DeviceIdType.MESH,
        )

    across = lax.rem(space + HALF // 2, SPACE)

    def near_peer(step):
        block, half = halves(space)
        return {"space": half * (HALF // 2) + lax.rem(block + step, HALF // 2)}

    def shared_refs():
        block, half = halves(space)
        for sender, side_of in ((space, half), (across, 1 - half)):
            yield (
                held_source.at[block, pl.ds(pl.multiple_of(side_of * 8, 8), 8)],
                held_wanted.at[sender],
            )

    def relays():
        return [
            remote(origin, target, relay_send.at[kind], relay_recv.at[kind], {"space": across})
            for kind, (origin, target) in enumerate(piece_refs(space)[1:])
        ]

    def send_sums(turn, norm, product):
        norm = norm + pltpu.roll(norm, 64, 1)
        product = product + pltpu.roll(product, 64, 1)
        both = jnp.where(lane < 64, norm, product)
        tiles[turn, member] = both[:4] + both[4:]
        for step in range(1, TEAM):
            tile_copy(turn, step).start()

    def sums_here(turn):
        wait_bytes(tiles.at[turn, pl.ds(0, TEAM - 1)], tile_recv.at[turn])
        both = jnp.sum(tiles[turn], axis=0)
        both = jnp.concatenate([both, both])
        norm = jnp.sum(jnp.where(lane < 64, both, 0.0), axis=1, keepdims=True)
        product = jnp.sum(jnp.where(lane < 64, 0.0, both), axis=1, keepdims=True)
        return jnp.broadcast_to(norm, plane), jnp.broadcast_to(product, plane)

    def over_rows(body, start):
        def several(group, carry):
            for i in range(4):
                for k in range(2):
                    carry = body(4 * group + i, k, carry)
            return carry

        return lax.fori_loop(0, HALF // 8, several, start)

    wanted[...] = jnp.broadcast_to(obs_row[...], wanted.shape)
    barrier = pltpu.get_barrier_semaphore()
    for step in range(1, SPACE):
        pl.semaphore_signal(barrier, inc=1, device_id=space_peer(step)[1], device_id_type=pl.DeviceIdType.MESH)
    for step in range(1, TEAM):
        pl.semaphore_signal(barrier, inc=1, device_id=team_peer(step), device_id_type=pl.DeviceIdType.MESH)
    for peer in sum_peers()[1]:
        for step in range(1, WIDE):
            pl.semaphore_signal(barrier, inc=1, device_id=peer(step)[1], device_id_type=pl.DeviceIdType.MESH)
    own = [
        pltpu.make_async_copy(origin, target, own_sems.at[kind])
        for kind, (origin, target) in enumerate(piece_refs(space))
    ]
    for copy in own:
        copy.start()
    pl.semaphore_wait(barrier, TEAM - 1 + SPACE - 1 + 3 * (WIDE - 1))
    for copy in relays():
        copy.start()
    for step in range(1, SPACE):
        other, device = space_peer(step)
        remote(*piece_refs(other)[0], swap_send.at[0], swap_recv.at[0], device).start()
    mine, theirs = shared_refs()
    for step in range(1, HALF // 2):
        for kind, target in enumerate(mine):
            origin = (source, wanted)[kind]
            remote(origin, target, swap_send.at[1 + kind], swap_recv.at[1 + kind], near_peer(step)).start()
    for copy in relays():
        copy.wait_recv()
    for step in range(1, HALF // 2):
        for kind, target in enumerate(theirs):
            remote(target, target, swap_send.at[1 + kind], swap_recv.at[1 + kind], near_peer(step)).start()

    @pl.when(member == 0)
    def _():
        source_edge[0] = jnp.zeros(source_edge.shape[1:], jnp.float32)
        for kind in range(ITERS - 1):
            edges[kind, 0] = jnp.zeros(edges.shape[2:], jnp.float32)

    @pl.when(member == TEAM - 1)
    def _():
        source_edge[1] = jnp.zeros(source_edge.shape[1:], jnp.float32)
        for kind in range(ITERS - 1):
            edges[kind, 1] = jnp.zeros(edges.shape[2:], jnp.float32)

    for copy in own:
        copy.wait()
    others = SPACE - 1
    wait_bytes(ensemble.at[pl.ds(0, others * 32)], swap_recv.at[0])
    wait_bytes(ensemble.at[pl.ds(0, (others - 1) * 8)], swap_recv.at[1])
    wait_bytes(held_wanted.at[pl.ds(0, others - 1)], swap_recv.at[2])

    def two_rows(lower, upper):
        return jnp.where(low_half, jnp.broadcast_to(lower, plane), jnp.broadcast_to(upper, plane))

    def close_ends(padded, outside):
        for y in range(4):
            first, last = padded[y, 1], padded[y, HALF]
            below = first if outside is None else outside
            above = last if outside is None else outside
            padded[y, 0] = jnp.where(low_half, below, pltpu.roll(last, 4, 0))
            padded[y, HALF + 1] = jnp.where(low_half, pltpu.roll(first, 4, 0), above)

    def begin(block, carry):
        rows = held_source[block]
        for k in range(2):
            for y in range(4):
                at = 4 * k + y
                held = held_rows[block, pl.ds(at, 8, stride=8), :]
                cond[y, 2 * block + k + 1] = jnp.exp(held)
                searched[y, 2 * block + k + 1] = two_rows(rows[at : at + 1], rows[8 + at : 9 + at])
        for upward in range(2):
            at = 3 * upward
            side[upward, block] = jnp.concatenate([rows[at + k : at + k + 1] for k in (0, 8, 4, 12)])
        return carry

    lax.fori_loop(0, HALF // 2, begin, 0)
    send_edges(COND)
    send_edges(SOURCE)
    close_ends(cond, None)
    close_ends(searched, jnp.zeros(plane, jnp.float32))

    @pl.when(member == 0)
    def _():
        cond_edge[0] = cond[0, pl.ds(1, HALF)]

    @pl.when(member == TEAM - 1)
    def _():
        cond_edge[1] = cond[3, pl.ds(1, HALF)]

    def inner_faces(block, k, carry):
        row = 2 * block + k
        here = cond[:, row + 1]
        face_x[:, row + 1] = harmonic(here, cond[:, row + 2])
        above = jnp.where(lane_4 == 127, here, pltpu.roll(here, 127, 2))
        upper = harmonic(here, above)
        face_z[:, row] = upper
        lower_z[:, row] = jnp.where(lane_4 == 0, here, pltpu.roll(upper, 1, 2))
        face_y[1:4, row] = harmonic(here[:3], here[1:])
        face_y[0, row] = here[0]
        face_y[4, row] = here[3]
        return carry

    over_rows(inner_faces, 0)
    for y in range(4):
        face_x[y, 0] = harmonic(cond[y, 0], cond[y, 1])

    def outer_faces(block, k, carry):
        row = 2 * block + k
        face_y[0, row] = harmonic(cond_edge[0, row], cond[0, row + 1])
        face_y[4, row] = harmonic(cond[3, row + 1], cond_edge[1, row])
        return carry

    def operate():
        def body(block, k, carry):
            row = 2 * block + k
            here = searched[:, row + 1]
            before = jnp.concatenate([here[:1], here[:3]])
            after = jnp.concatenate([here[1:], here[3:]])
            result = face_x[:, row + 1] * (here - searched[:, row + 2])
            result = result + face_x[:, row] * (here - searched[:, row])
            result = result + face_y[1:5, row] * (here - after)
            result = result + face_y[0:4, row] * (here - before)
            above = jnp.where(lane_4 == 127, 0.0, pltpu.roll(here, 127, 2))
            below = jnp.where(lane_4 == 0, 0.0, pltpu.roll(here, 1, 2))
            result = result + face_z[:, row] * (here - above)
            image[:, row] = result + lower_z[:, row] * (here - below)
            return carry

        over_rows(body, 0)

    def operate_edges(lower_edge, upper_edge):
        def body(block, k, carry):
            row = 2 * block + k
            image[0, row] = image[0, row] + face_y[0, row] * (searched[0, row + 1] - lower_edge(block, k))
            image[3, row] = image[3, row] + face_y[4, row] * (searched[3, row + 1] - upper_edge(block, k))
            return carry

        over_rows(body, 0)

    def over_planes(body, kind):
        def outer(block, k, carry):
            return body(slice(3, 4), 2 * block + k, body(slice(0, 1), 2 * block + k, carry))

        def inner(block, k, carry):
            return body(slice(1, 3), 2 * block + k, carry)

        sums = over_rows(outer, (zeros, zeros))
        if kind < ITERS - 1:
            send_edges(kind)
        return over_rows(inner, sums)

    zeros = jnp.zeros(plane, jnp.float32)
    operate()
    edges_here(COND)
    over_rows(outer_faces, 0)
    edges_here(SOURCE)

    def source_side(upward):
        def rows(block, k):
            four = source_edge[upward, block]
            return two_rows(four[2 * k : 2 * k + 1], four[2 * k + 1 : 2 * k + 2])

        return rows

    operate_edges(source_side(0), source_side(1))

    def first_sums(ys, row, carry):
        norm, product = carry
        image_here = image[ys, row]
        residual_here = searched[ys, row + 1]
        residual[ys, row] = residual_here
        searched[ys, row + 1] = image_here
        return norm + jnp.sum(residual_here * residual_here, axis=0), product + jnp.sum(
            residual_here * image_here, axis=0
        )

    norm, product = over_planes(first_sums, 0)

    norm_before = step_before = None
    for turn in range(ITERS):
        last = turn == ITERS - 1
        send_sums(turn, norm, product)
        if not last:
            close_ends(searched, zeros)
            operate()
            edges_here(turn)
            operate_edges(
                lambda block, k: edges[turn, 0, 2 * block + k], lambda block, k: edges[turn, 1, 2 * block + k]
            )
        norm_now, product_now = sums_here(turn)
        if turn == 0:
            step_size = norm_now / product_now
        else:
            ratio = norm_now / norm_before
            step_size = norm_now / (product_now - ratio * norm_now / step_before)
        norm_before, step_before = norm_now, step_size

        def update(ys, row, carry):
            norm, product = carry
            residual_here, image_here = residual[ys, row], searched[ys, row + 1]
            direction_here, along_here, beyond_here = residual_here, image_here, image[ys, row]
            answer_here = step_size * direction_here
            if turn > 0:
                direction_here = direction_here + ratio * direction[ys, row]
                along_here = along_here + ratio * along[ys, row]
                beyond_here = beyond_here + ratio * beyond[ys, row]
                answer_here = answer[ys, row] + step_size * direction_here
            residual_here = residual_here - step_size * along_here
            image_here = image_here - step_size * beyond_here
            answer[ys, row] = answer_here
            direction[ys, row] = direction_here
            along[ys, row] = along_here
            beyond[ys, row] = beyond_here
            residual[ys, row] = residual_here
            searched[ys, row + 1] = image_here
            return norm + jnp.sum(residual_here * residual_here, axis=0), product + jnp.sum(
                residual_here * image_here, axis=0
            )

        def finish(block, k, carry):
            row = 2 * block + k
            answer[:, row] = answer[:, row] + step_size * (residual[:, row] + ratio * direction[:, row])
            return carry

        if last:
            over_rows(finish, 0)
        else:
            edges_sent(turn)
            norm, product = over_planes(update, turn + 1)

    for block in range(HALF // 2):
        chosen = two_rows(held_wanted[block], held_wanted[HALF // 2 + block])
        value = zeros
        for choice in range(8):
            value = value + jnp.where(chosen == choice, answer[choice % 4, 2 * block + choice // 4], 0.0)
        picked[block] = value[:4]
        picked[HALF // 2 + block] = value[4:]

    returned[space] = picked[space]
    for step in range(1, SPACE):
        other, device = space_peer(step)
        pltpu.make_async_remote_copy(
            src_ref=picked.at[other],
            dst_ref=returned.at[space],
            send_sem=swap_send.at[3],
            recv_sem=swap_recv.at[3],
            device_id=device,
            device_id_type=pl.DeviceIdType.MESH,
        ).start()
    wait_bytes(returned.at[pl.ds(0, others)], swap_recv.at[3])
    for i in range(SPACE // 2):
        predicted[pl.ds(8 * i, 8)] = jnp.concatenate([returned[2 * i], returned[2 * i + 1]])

    values = predicted[...]
    inverse_sigma = 1.0 / jnp.sqrt(obs_var[...])
    spread = (values - jnp.mean(values, axis=0, keepdims=True)) * inverse_sigma
    misfit = (obs_values[...] - values) * inverse_sigma + obs_noise[...]
    for i, other in enumerate((spread, misfit)):
        product = lax.dot_general(
            spread, other, (((1,), (1,)), ((), ())), precision=lax.Precision.HIGHEST, preferred_element_type=jnp.float32
        )
        for j in range(HALF):
            part[HALF * i + j] = product[4 * j : 4 * j + 4]
    sum_everywhere(part, total, *sum_refs)

    edges_sent(COND)
    edges_sent(SOURCE)
    for turn in range(ITERS):
        wait_bytes(tiles.at[turn, pl.ds(0, TEAM - 1)], tile_send.at[turn])
    wait_bytes(ensemble.at[pl.ds(0, others * 32)], swap_send.at[0])
    wait_bytes(ensemble.at[pl.ds(0, (others - 1) * 8)], swap_send.at[1])
    wait_bytes(held_wanted.at[pl.ds(0, others - 1)], swap_send.at[2])
    wait_bytes(returned.at[pl.ds(0, others)], swap_send.at[3])
    for copy in relays():
        copy.wait_send()


def predict(ensemble, source, obs_row, obs_values, obs_noise, obs_var):
    held = (4, HALF, 8, 128)
    padded = (4, HALF + 2, 8, 128)
    vmem = lambda *shape: pltpu.VMEM(shape, jnp.float32)
    return pl.pallas_call(
        conjugate_kernel,
        out_shape=[jax.ShapeDtypeStruct((rows, 128), jnp.float32) for rows in (128, 256)],
        in_specs=[pl.BlockSpec(memory_space=pl.ANY), *[pl.BlockSpec(memory_space=pltpu.VMEM)] * 5],
        out_specs=[pl.BlockSpec(memory_space=pltpu.VMEM)] * 2,
        scratch_shapes=[
            pltpu.VMEM((1, 128), jnp.int32),
            vmem(HALF // 2, 64, 128),
            vmem(HALF // 2, 16, 128),
            pltpu.VMEM((SPACE, 1, 128), jnp.int32),
            vmem(SPACE, 4, 128),
            vmem(SPACE, 4, 128),
            vmem(2, HALF // 2, 4, 128),
            vmem(*padded),
            vmem(4, HALF + 1, 8, 128),
            vmem(5, HALF, 8, 128),
            vmem(*held),
            vmem(*held),
            vmem(*padded),
            *[vmem(*held)] * 6,
            vmem(2, HALF, 8, 128),
            vmem(2, HALF // 2, 4, 128),
            vmem(ITERS - 1, 2, HALF, 8, 128),
            vmem(ITERS, TEAM, 4, 128),
            pltpu.SemaphoreType.DMA((ITERS + 1, 2)),
            pltpu.SemaphoreType.DMA((ITERS + 1, 2)),
            pltpu.SemaphoreType.DMA((ITERS,)),
            pltpu.SemaphoreType.DMA((ITERS,)),
            pltpu.SemaphoreType.DMA((4,)),
            pltpu.SemaphoreType.DMA((4,)),
            pltpu.SemaphoreType.DMA((3,)),
            pltpu.SemaphoreType.DMA((2,)),
            pltpu.SemaphoreType.DMA((2,)),
            vmem(64, 4, 128),
            vmem(WIDE - 1, WIDE, 4, 128),
            vmem(WIDE, 4, 128),
            vmem(WIDE - 1, 4, 128),
            vmem(4, 128),
            vmem(WIDE, 4, 128),
            vmem(WIDE, 4, 128),
            vmem(WIDE, WIDE, 4, 128),
            pltpu.SemaphoreType.DMA((5, WIDE - 1)),
            pltpu.SemaphoreType.DMA((5, WIDE - 1)),
        ],
        compiler_params=pltpu.CompilerParams(collective_id=2, has_side_effects=True),
        name="predict",
    )(ensemble, source, obs_row, obs_values, obs_noise, obs_var)


PANEL, GROUP = 8, 32


def solve_kernel(total, ensemble, values, updated, predicted, gram, cross, scaled, weights):
    plane = (PANEL, 128)
    count = gram.shape[0]
    sublane = lax.broadcasted_iota(jnp.int32, plane, 0)
    lane = lax.broadcasted_iota(jnp.int32, plane, 1)
    whole = functools.partial(lax.dot_general, precision=lax.Precision.HIGHEST, preferred_element_type=jnp.float32)

    def spread(row):
        return jnp.broadcast_to(row, plane)

    predicted[...] = values[...]
    for low in range(0, count, PANEL):
        gram[low : low + PANEL] = total[low : low + PANEL] + jnp.where(lane == sublane + low, count - 1.0, 0.0)
    cross[...] = total[count:]

    for low in range(0, count, PANEL):
        first = low - low % GROUP
        rows_g, rows_c = gram[low : low + PANEL], cross[low : low + PANEL]
        for k in range(first, low):
            if k % PANEL == 0:
                held = rows_g
            ahead = spread(held[:, k : k + 1])
            rows_g = rows_g - ahead * spread(scaled[k : k + 1])
            rows_c = rows_c - ahead * spread(weights[k : k + 1])
        gram[low : low + PANEL] = rows_g
        columns = [spread(rows_g[:, low + j : low + j + 1]) for j in range(PANEL)]
        pivots = {(i, j): spread(columns[j][i : i + 1]) for j in range(PANEL) for i in range(j + 1)}
        inverse, factor = [], {}
        for k in range(PANEL):
            inverse.append(1.0 / pivots[k, k])
            for i in range(k + 1, PANEL):
                factor[i, k] = pivots[k, i] * inverse[k]
                for j in range(i, PANEL):
                    pivots[i, j] = pivots[i, j] - factor[i, k] * pivots[k, j]
        solved = []
        for rows in (rows_g, rows_c):
            lines = [spread(rows[i : i + 1]) for i in range(PANEL)]
            for k in range(PANEL):
                for i in range(k + 1, PANEL):
                    lines[i] = lines[i] - factor[i, k] * lines[k]
            lines = [line * inverse[i] for i, line in enumerate(lines)]
            for k in reversed(range(PANEL)):
                for i in range(k):
                    lines[i] = lines[i] - factor[k, i] * lines[k]
            joined = lines[0]
            for i in range(1, PANEL):
                joined = jnp.where(sublane == i, lines[i], joined)
            solved.append(joined)
        scaled[low : low + PANEL] = solved[0]
        weights[low : low + PANEL] = solved[1]
        after = low + PANEL
        if after % GROUP == 0 and after < count:
            taken = gram[first:after].T
            for target, factors in ((gram, scaled), (cross, weights)):
                change = whole(taken, factors[first:after], (((1,), (0,)), ((), ())))
                target[after:] = target[after:] - change[after:]

    for first in range(count - GROUP, -1, -GROUP):
        group = slice(first, first + GROUP)
        if first + GROUP < count:
            later = lax.broadcasted_iota(jnp.int32, (GROUP, count), 1) >= first + GROUP
            left = jnp.where(later, scaled[group], 0.0)
            weights[group] = weights[group] - whole(left, weights[...], (((1,), (0,)), ((), ())))
        for low in range(first + GROUP - 2 * PANEL, first - 1, -PANEL):
            rows_g, rows_c = scaled[low : low + PANEL], weights[low : low + PANEL]
            for k in range(low + PANEL, first + GROUP):
                rows_c = rows_c - spread(rows_g[:, k : k + 1]) * spread(weights[k : k + 1])
            weights[low : low + PANEL] = rows_c

    turned = weights[...].T
    for row in range(PANEL):
        picks = [pl.ds(row + 8 * PANEL * i, PANEL, stride=8) for i in range(count // PANEL)]
        fields = [ensemble[pick, :] for pick in picks]
        mean = jnp.sum(sum(fields), axis=0, keepdims=True) * (1.0 / count)
        change = whole(turned, jnp.concatenate([field - mean for field in fields]), (((1,), (0,)), ((), ())))
        for i, pick in enumerate(picks):
            updated[pick, :] = fields[i] + change[PANEL * i : PANEL * (i + 1)]


def solve_and_update(total, ensemble, values):
    square = pltpu.VMEM((total.shape[1], total.shape[1]), jnp.float32)
    return pl.pallas_call(
        solve_kernel,
        out_shape=[jax.ShapeDtypeStruct(array.shape, jnp.float32) for array in (ensemble, values)],
        in_specs=[pl.BlockSpec(memory_space=pltpu.VMEM)] * 3,
        out_specs=[pl.BlockSpec(memory_space=pltpu.VMEM)] * 2,
        scratch_shapes=[square] * 4,
        name="solve_and_update",
    )(total, ensemble, values)


def local(ensemble, source, obs_rows, obs_values, obs_noise, obs_var):
    layers = source.shape[-1]
    fields = ensemble.reshape(-1, layers)
    predicted, total = predict(
        fields,
        source.reshape(-1, layers),
        obs_rows.reshape(1, 1),
        obs_values.reshape(1, layers),
        obs_noise.reshape(-1, layers),
        obs_var.reshape(1, layers),
    )
    updated, predicted = solve_and_update(total, fields, predicted)
    return (updated.reshape(ensemble.shape), predicted.reshape(obs_noise.shape))


def solution(mesh):
    in_specs = (
        P(None, "space", "member", None),
        P("space", "member", None),
        P("space", "member", None),
        P("space", "member", None),
        P(None, "space", "member", None),
        P("space", "member", None),
    )
    out_specs = (P(None, "space", "member", None), P(None, "space", "member", None))
    return jax.shard_map(local, mesh=mesh, in_specs=in_specs, out_specs=out_specs, check_vma=False)
```
